32 devices in a mesh: front: 4 (over z), row: 4 (over x, core), col: 2 (over y).
Axes of the slice: x: 2, y: 2, z: 4, core: 2. Of those that a mesh axis runs over, the one named last changes fastest.
Arguments:
- front_slab: bfloat16 [4, 2048, 8192], P('front', 'row', 'col'), may hold values from -0.0625 to 0.0625
- samples: bfloat16 [8192, 256], P(('row', 'col')), may hold values from -6 to 6
- child_tiles: bfloat16 [64, 128, 2048], P(('front', 'row', 'col')), may hold values from -0.125 to 0.125
- parent_front: int32 [64, 1], P(('front', 'row', 'col')), may hold values from 0 to 3; in each aligned block of 2 rows (0 to 1, 2 to 3, ...) at most 2 rows name the same one
- parent_tile: int32 [64], P(('front', 'row', 'col')), may hold values from 0 to 15
- column_tiles: int32 [64, 16], P(('front', 'row', 'col')), may hold values from 0 to 63
- ranks: int32 [4, 4], P('front', 'row'), may hold values from 128 to 256
Outputs:
- sampled: float32 [4, 2048, 256], P('front', ('row', 'col'))
- bases: float32 [4, 2048, 256], P('front', ('row', 'col'))
The draws below stay inside these ranges and needn't reach their ends.
Inputs may be any that keep to these rules, and one draw needn't show every extreme that they name: `parent_front`: among the 2 tiles of one device, at most 2 name the same parent front.
All inputs are finite; a program needn't handle non-finite values.
Results may differ from the reference program's by a relative error of at most 0.0003.
Values may be sent and summed in bfloat16 or wider, within the bound.
A program may use at most 64 MiB of HBM per device.

```python
import math
import jax
import jax.numpy as jnp
import numpy as np
from jax import lax

F = 8192
S = 256
LEAF = 512
CW = 2048
TILE_DEV = 2
ROWS = 2048
ROW_TILES = 16
PARENTS = 4
CAP = 2
TILES = 64
N_ROW = 4
N_COL = 2


def touch_ends(result, stream_key, low, largest):
    longest = result.shape.index(max(result.shape))
    spots = []
    for shift in (0, 1):
        where = [jax.random.randint(jax.random.fold_in(stream_key, axis), (), 0, length) for axis, length in enumerate(result.shape)]
        where[longest] = (where[longest] + shift) % result.shape[longest]
        spots.append(tuple(where))
    return result.at[spots[0]].set(low).at[spots[1]].set(largest)


def shard_levels(rng, extent, cuts, smallest, largest):
    factor_of, own = 1.0, jax.random.fold_in(rng, 6)
    for axis_at, parts in cuts:
        heights = jnp.exp(jax.random.uniform(jax.random.fold_in(own, axis_at), (parts,), jnp.float32, smallest / len(cuts), largest / len(cuts)))
        factor_of = factor_of * jnp.repeat(heights, extent[axis_at] // parts).reshape([-1 if axis == axis_at else 1 for axis in range(len(extent))])
    return factor_of


def routed_block(stream_key, own, number, rows, amount, top, reach, lean):
    ranking = jax.random.permutation(stream_key, amount)
    packed, ordinary = portions_of(amount, rows * top, reach, lean, True), portions_of(amount, rows * top, reach, lean, False)
    places = jnp.arange(amount)

    def named(sizes, offset_by):
        used = int((sizes > 0).sum())
        fixed = max(1, used // 4)
        shifted = fixed + (places - fixed + offset_by * (used - fixed)) % max(1, amount - fixed)
        return jnp.zeros((amount,), jnp.int32).at[ranking[jnp.where(places < fixed, places, shifted)]].set(jnp.asarray(sizes, jnp.int32))

    sizes = jnp.where(number % 4 == 0, named(packed, number // 4), named(ordinary, number - number // 4 - 1))
    mixed = jax.random.permutation(jax.random.fold_in(own, 3), amount)
    source_of, taker = mixed[0:amount // 2 * 2:2], mixed[1:amount // 2 * 2:2]
    margin = jnp.minimum(sizes[source_of] - 1, reach - sizes[taker]) // 2
    margin = jnp.where((source_of == ranking[0]) | (taker == ranking[0]) | (sizes[taker] == 0), 0, jnp.maximum(margin, 0))
    shifted = jax.random.randint(jax.random.fold_in(own, 4), (amount // 2,), 0, 1 << 20) % (margin + 1)
    sizes = sizes.at[source_of].add(-shifted).at[taker].add(shifted)
    items = jnp.searchsorted(jnp.cumsum(sizes), jnp.arange(rows * top), side="right").astype(jnp.int32)
    grid = items.reshape(top, rows).T
    grid = grid[jax.random.permutation(jax.random.fold_in(own, 1), rows)]
    offset_by = jax.random.randint(jax.random.fold_in(own, 2), (rows, 1), 0, top)
    return jnp.take_along_axis(grid, (jnp.arange(top)[None, :] + offset_by) % top, axis=1)


def portions_of(count, total, most, lean, full):
    loads = [(1 << 20) // math.isqrt(standing ** lean) + 1 for standing in range(1, count + 1)]
    largest = most if full else min(most, max(-(-total // count), total * loads[0] // sum(loads)))
    least = 1 if total - largest >= count - 1 else 0
    holding, surplus = [largest] + [least] * (count - 1), total - largest - least * (count - 1)
    while surplus > 0:
        candidates = [i for i in range(1, count) if holding[i] < largest] or [i for i in range(1, count) if holding[i] < most]
        whole, budget = sum([loads[i] for i in candidates]), surplus
        for i in candidates:
            addition = min(most - holding[i], max(1, budget * loads[i] // whole), surplus)
            holding[i] = holding[i] + addition
            surplus = surplus - addition
    return np.array(holding)


def normal_values(key, extent, scale, most, cuts=(), kind=jnp.bfloat16):
    array = jax.random.normal(key, extent, jnp.float32) * scale
    if len(cuts) > 0:
        array = shard_levels(key, extent, cuts, -0.22, 0.18) * array
    return jnp.clip(array, min=-most, max=most).astype(kind)


def setup_inputs(seed: int = 0) -> dict:
    key_list = jax.random.split(jax.random.key(seed), 8)
    front_slab = normal_values(key_list[0], (PARENTS, ROWS, F), F ** -0.5, 0.0625, ((0, 4), (1, 4), (2, 2)))
    samples = normal_values(key_list[1], (F, S), 1.0, 6.0, ((0, 8),))
    child_tiles = normal_values(key_list[2], (TILES, 128, CW), (CW * TILE_DEV * N_ROW * N_COL // ROW_TILES) ** -0.5, 0.125, ((0, 32),))
    parent_front_keys = jax.random.split(jax.random.fold_in(key_list[3], 1), TILES // TILE_DEV)
    parent_front_turns = jax.random.permutation(jax.random.fold_in(key_list[3], 3), TILES // TILE_DEV)
    parent_front = jax.vmap(lambda own, number: routed_block(jax.random.fold_in(key_list[3], 2), own, number, TILE_DEV, PARENTS, 1, CAP, 2))(parent_front_keys, parent_front_turns).reshape((TILES, 1))
    parent_tile = touch_ends(jax.random.randint(key_list[4], (TILES,), 0, ROW_TILES), jax.random.fold_in(key_list[4], 1), 0, ROW_TILES - 1).astype(jnp.int32)
    column_tiles = touch_ends(jax.random.randint(key_list[5], (TILES, CW // 128), 0, F // 128), jax.random.fold_in(key_list[5], 1), 0, (F // 128) - 1).astype(jnp.int32)
    ranks = touch_ends(jax.random.randint(key_list[6], (PARENTS, N_ROW), S // 2, S + 1), jax.random.fold_in(key_list[6], 1), S // 2, S).astype(jnp.int32)
    return dict(front_slab=front_slab, samples=samples, child_tiles=child_tiles, parent_front=parent_front, parent_tile=parent_tile, column_tiles=column_tiles, ranks=ranks)


def leaf_basis(block, rank):
    width = block.shape[1]
    mask = (jnp.arange(width, dtype=jnp.int32) < rank).astype(jnp.float32)
    masked = block * mask[None, :]
    gram = jnp.dot(masked.T, masked, precision=lax.Precision.HIGHEST)
    gram = gram + jnp.diag(1.0 - mask)
    lower = jnp.linalg.cholesky(gram)
    return lax.linalg.triangular_solve(lower, masked, left_side=False, lower=True, transpose_a=True)

def reference(front_slab, samples, child_tiles, parent_front, parent_tile, column_tiles, ranks):
    parents = front_slab.shape[0]
    rows = front_slab.shape[1]
    full = front_slab.shape[2]
    width = samples.shape[1]
    tile_cols = child_tiles.shape[2]
    blocks = tile_cols // 128
    row_tiles = rows // 128
    omega_tiles = samples.reshape(full // 128, 128, width)
    devices = child_tiles.shape[0] // TILE_DEV
    tiles_blk = child_tiles.reshape(devices, TILE_DEV, 128, blocks, 128)
    dest_blk = parent_front.reshape(devices, TILE_DEV)
    place_blk = parent_tile.reshape(devices, TILE_DEV)
    cols_blk = column_tiles.reshape(devices, TILE_DEV, blocks)

    def step(acc, item):
        pieces, dest, place, cols = item
        chosen = omega_tiles[cols].astype(jnp.float32)
        product = jnp.einsum('trkc,tkcs->trs', pieces.astype(jnp.float32), chosen)
        key = (dest * row_tiles + place).astype(jnp.int32)
        return (acc.at[key].add(product), None)
    start = jnp.zeros((parents * row_tiles, 128, width), jnp.float32)
    extended, _ = lax.scan(step, start, (tiles_blk, dest_blk, place_blk, cols_blk))
    direct = lax.map(lambda slab: jnp.dot(slab.astype(jnp.float32), samples.astype(jnp.float32), preferred_element_type=jnp.float32), front_slab)
    sampled = direct + extended.reshape(parents, rows, width)
    leaves = sampled.reshape(parents * N_ROW, LEAF, width)
    bases = jax.vmap(leaf_basis)(leaves, ranks.reshape(-1))
    return (sampled, bases.reshape(parents, rows, width))
```

```python
import functools

import jax
import jax.numpy as jnp
from jax import lax
from jax.experimental import pallas as pl
from jax.experimental.pallas import tpu as pltpu
from jax.sharding import PartitionSpec as P

F32 = jnp.float32
HI = lax.Precision.HIGHEST
LOGICAL = pl.DeviceIdType.MESH


def dot_nt(a, b):
    return lax.dot_general(a, b, (((1,), (1,)), ((), ())), precision=HI, preferred_element_type=F32)


def inverse_factor(a):
    n = a.shape[0]
    tiles = n // 8
    w = [a[8 * t : 8 * t + 8, :] for t in range(tiles)]
    lane = lax.broadcasted_iota(jnp.int32, (8, n), 1)
    sub = lax.broadcasted_iota(jnp.int32, (8, n), 0)
    rows = []
    for t in range(tiles):
        base = 8 * t
        inside = (lane >= base) & (lane < base + 8)
        cols = [jnp.broadcast_to(w[t][:, base + k : base + k + 1], (8, n)) for k in range(8)]
        v = jnp.where(inside, jnp.where(lane - base == sub, 1.0, 0.0), w[t])
        done, pivots = v, cols[0]
        for k in range(8):
            here = sub == k
            pivot = jnp.broadcast_to(cols[k][k : k + 1, :], (8, n))
            inv = 1.0 / pivot
            done = jnp.where(here, v, done)
            pivots = jnp.where(here, pivot, pivots)
            step = jnp.broadcast_to(v[k : k + 1, :], (8, n)) * inv
            v = jnp.where(here, step, v - cols[k] * step)
            for m in range(k + 1, 8):
                step = jnp.broadcast_to(cols[m][k : k + 1, :], (8, n)) * inv
                cols[m] = jnp.where(here, step, cols[m] - cols[k] * step)
        rows.append(jnp.where(lane < base + 8, done, 0.0) * lax.rsqrt(pivots))
        vk = [jnp.broadcast_to(v[k : k + 1, :], (8, n)) for k in range(8)]
        for u in range(t + 1, tiles):
            x = jnp.where(inside, 0.0, w[u])
            terms = [
                jnp.broadcast_to(w[u][:, base + k : base + k + 1], (8, n)) * vk[k] for k in range(8)
            ]
            low = (terms[0] + terms[1]) + (terms[2] + terms[3])
            high = (terms[4] + terms[5]) + (terms[6] + terms[7])
            w[u] = x - (low + high)
    return jnp.concatenate(rows, axis=0)


def basis_kernel(sampled_ref, gram_ref, out_ref, basis_ref):
    half = gram_ref.shape[2]
    rank = gram_ref[0, half : half + 1, :]
    sampled = sampled_ref[...]
    out_ref[...] = sampled
    rows = sampled.shape[0]
    lane = lax.broadcasted_iota(jnp.int32, (rows, half), 1).astype(F32)
    first = jnp.where(lane < rank, sampled[:, :half], 0.0)
    second = jnp.where(lane + half < rank, sampled[:, half:], 0.0)
    r = lax.broadcasted_iota(jnp.int32, (half, half), 0)
    c = lax.broadcasted_iota(jnp.int32, (half, half), 1)
    lane = c.astype(F32)
    a = gram_ref[0, :half, :] + jnp.where((r == c) & (lane >= rank), 1.0, 0.0)
    inv1 = inverse_factor(a)
    low = dot_nt(gram_ref[1, :half, :], inv1)
    a = gram_ref[2, :half, :] + jnp.where((r == c) & (lane + half >= rank), 1.0, 0.0)
    a = a - dot_nt(low, low)
    inv2 = inverse_factor(a)
    basis = dot_nt(first, inv1)
    basis_ref[:, :half] = basis
    basis_ref[:, half:] = dot_nt(second - dot_nt(basis, low), inv2)


def leaf_bases(sampled, gram):
    vmem = pl.BlockSpec(memory_space=pltpu.VMEM)
    return pl.pallas_call(
        basis_kernel,
        out_shape=(jax.ShapeDtypeStruct(sampled.shape, F32),) * 2,
        in_specs=[vmem, vmem],
        out_specs=(vmem, vmem),
        name="leaf_bases",
    )(sampled, gram)


LEVELS = 32767.0


def widened(code):
    return code.astype(jnp.int32).astype(F32)


def step_of(code):
    return jnp.exp2(widened(code) * (1.0 / 256.0)) * (1.0 / LEVELS)


def code_of(block):
    peak = jnp.max(jnp.max(jnp.abs(block), axis=0, keepdims=True), axis=1, keepdims=True)
    peak = jnp.broadcast_to(jnp.maximum(peak, 1e-30), (8, 128))
    return jnp.ceil(jnp.log2(peak) * 256.0) + 2.0


def coded(block, code):
    rows, lanes = block.shape
    scale = jnp.exp2(code * (-1.0 / 256.0)) * LEVELS
    scaled = (block.reshape(rows // 8, 8, lanes) * scale[None]).reshape(rows, lanes)
    return jnp.round(scaled).astype(jnp.int32).astype(jnp.int16)


def decoded(words, step):
    rows, lanes = words.shape
    values = widened(words).reshape(rows // 8, 8, lanes) * step[None]
    return values.reshape(rows, lanes)


def sample_kernel(
    fronts,
    tile_hbm,
    front_hbm,
    column_hbm,
    rank_hbm,
    slab_ref,
    samples_ref,
    child_ref,
    sampled_ref,
    gram_ref,
    tile_ref,
    front_ref,
    column_ref,
    rank_ref,
    omega,
    slab,
    child,
    labels,
    label_ref,
    held,
    sums,
    part,
    blocks,
    got,
    gram_own,
    gram_got,
    copy_sem,
    gs,
    gr,
    zs_right,
    zs_left,
    zs_pair,
    zr,
    zr_pair,
    es,
    er,
):
    f, r, c = lax.axis_index("front"), lax.axis_index("row"), lax.axis_index("col")
    x, core = r // 2, r % 2
    width = samples_ref.shape[2]
    half = width // 2
    chunk = samples_ref.shape[0]
    piece = chunk // 8
    odd = f % 2
    count = child_ref.shape[0]
    slab_rows, slab_cols = slab_ref.shape
    own_rows = slab_rows // 2
    pieces = own_rows // 128
    row_tiles = slab_rows * 4 // 128
    head = 8 * count
    r_x = (1 - x) * 2 + core
    r_p = x * 2 + (1 - core)
    r_d = (1 - x) * 2 + (1 - core)
    to_x, to_y, to_p, to_d = (f, r_x, c), (f, r, 1 - c), (f, r_p, c), (f, r_x, 1 - c)
    right, left = (f + 1, r, c), (f - 1, r, c)
    to_z = (f + 1 - 2 * odd, r, c)

    loads = [
        pltpu.make_async_copy(child_ref, child, copy_sem.at[0]),
        pltpu.make_async_copy(slab_ref, slab, copy_sem.at[1]),
        pltpu.make_async_copy(
            samples_ref, omega.at[pl.ds((r * 2 + c) * chunk, chunk)], copy_sem.at[2]
        ),
    ]
    small = [
        pltpu.make_async_copy(src, dst, copy_sem.at[3 + n])
        for n, (src, dst) in enumerate(
            (
                (tile_hbm, tile_ref),
                (front_hbm, front_ref),
                (column_hbm, column_ref),
                (rank_hbm, rank_ref),
            )
        )
    ]
    loads[2].start()
    for cp in small:
        cp.start()
    loads[0].start()
    loads[1].start()

    barrier = pltpu.get_barrier_semaphore()
    for target in (to_x, to_y, to_p, to_d):
        pl.semaphore_signal(barrier, inc=1, device_id=target, device_id_type=LOGICAL)

    @pl.when(f < fronts - 1)
    def _():
        pl.semaphore_signal(barrier, inc=1, device_id=right, device_id_type=LOGICAL)

    @pl.when(f > 0)
    def _():
        pl.semaphore_signal(barrier, inc=1, device_id=left, device_id_type=LOGICAL)

    pl.semaphore_wait(barrier, 4 + jnp.minimum(f, 1) + jnp.minimum(fronts - 1 - f, 1))

    def rcopy(src, dst, send, recv, target):
        return pltpu.make_async_remote_copy(
            src_ref=src,
            dst_ref=dst,
            send_sem=send,
            recv_sem=recv,
            device_id=target,
            device_id_type=LOGICAL,
        )

    def spot(i):
        return (i + odd * (7 - 2 * i)) * piece

    def place(row, col, i):
        return omega.at[pl.ds((row * 2 + col) * chunk + spot(i), piece)]

    sent = []

    def send(ref, n, target, src=None):
        cp = rcopy(ref if src is None else src, ref, gs.at[n], gr.at[n], target)
        cp.start()
        sent.append(cp)

    def arrived(ref, n):
        rcopy(ref, ref, gs.at[n], gr.at[n], to_p).wait_recv()

    def own(i):
        return samples_ref.at[pl.ds(spot(i), piece)]

    x_at = functools.partial(place, r_x, c)
    y_at = functools.partial(place, r, 1 - c)
    d_at = functools.partial(place, r_x, 1 - c)

    for i in range(5):
        send(place(r, c, i), i, to_x, own(i))
        send(place(r, c, 7 - i), 5 + i, to_y, own(7 - i))
    mine = omega.at[pl.ds((r * 2 + c) * chunk, chunk)]
    send(mine, 24, to_p, samples_ref)

    def view(ch, side, src):
        return labels.at[side, src] if ch == 2 else held.at[ch, side, src]

    def along(src, ch, sem, target):
        ref = view(ch, 0, src)
        return rcopy(ref, ref, sem.at[ch, src], zr.at[ch, src], target)

    def across(src, ch):
        return rcopy(
            view(ch, 0, src), view(ch, 1, src), zs_pair.at[ch, src], zr_pair.at[ch, src], to_p
        )

    def launch(ch):
        @pl.when(f < fronts - 1)
        def _():
            along(f, ch, zs_right, right).start()

        @pl.when(f > 0)
        def _():
            along(f, ch, zs_left, left).start()

        across(f, ch).start()

    def relay(ch, d):
        @pl.when(f >= d)
        def _():
            along(f - d, ch, zs_right, right).wait_recv()

            @pl.when(f < fronts - 1)
            def _():
                along(f - d, ch, zs_right, right).start()

            across(f - d, ch).start()

        @pl.when(f + d < fronts)
        def _():
            along(f + d, ch, zs_left, left).wait_recv()

            @pl.when(f > 0)
            def _():
                along(f + d, ch, zs_left, left).start()

            across(f + d, ch).start()

    def paired(ch):
        for s in range(fronts):
            across(s, ch).wait_recv()

    def drained(ch):
        for s in range(fronts):
            across(s, ch).wait_send()

            @pl.when((f < fronts - 1) & (f >= s))
            def _():
                along(s, ch, zs_right, right).wait_send()

            @pl.when((f > 0) & (f <= s))
            def _():
                along(s, ch, zs_left, left).wait_send()

    for cp in small:
        cp.wait()
    at_row = lax.broadcasted_iota(jnp.int32, (8, 128), 0)
    own_labels = jnp.zeros((8, 128), jnp.int32)
    for t in range(count):
        label = front_ref[t] * row_tiles + tile_ref[t]
        own_labels = jnp.where(at_row == t, label, own_labels)
    labels[0, f] = own_labels
    launch(2)

    for i in range(5):
        arrived(x_at(i), i)
        if i < 3:
            send(x_at(i), 18 + i, to_z)
        if i < 4:
            send(x_at(i), 14 + i, to_y)
        send(x_at(i), 25 + i, to_p)
        arrived(y_at(7 - i), 5 + i)
        if i < 3:
            send(y_at(7 - i), 21 + i, to_z)
        if i < 4:
            send(y_at(7 - i), 10 + i, to_x)
        send(y_at(7 - i), 33 + 7 - i, to_p)
        if 1 <= i < fronts:
            relay(2, i)
    for i in range(3):
        arrived(x_at(7 - i), 18 + i)
        send(x_at(7 - i), 25 + 7 - i, to_p)
        arrived(y_at(i), 21 + i)
        send(y_at(i), 33 + i, to_p)
    for d in range(5, fronts):
        relay(2, d)
    paired(2)
    to_smem = pltpu.make_async_copy(labels, label_ref, copy_sem.at[7])
    to_smem.start()
    for i in range(4):
        arrived(d_at(7 - i), 10 + i)
        send(d_at(7 - i), 41 + 7 - i, to_p)
        arrived(d_at(i), 14 + i)
        send(d_at(i), 41 + i, to_p)
    to_smem.wait()

    sources = [(side, s, t) for s in range(fronts) for side in range(2) for t in range(count)]
    none = len(sources)
    known = [label_ref[side, s, t, 0] for side, s, t in sources]
    before = []
    for n, label in enumerate(known):
        prev = jnp.int32(none)
        for m in range(n):
            prev = jnp.where(known[m] == label, m, prev)
        before.append(prev)

    def last_of(row, col, j):
        wanted = f * row_tiles + (row * 2 + col) * pieces + j
        last = jnp.int32(none)
        for n, label in enumerate(known):
            last = jnp.where(label == wanted, n, last)
        return last

    spots = [(r_x, 1 - c), (r_x, c), (r, 1 - c), (r, c)]
    lasts = [[last_of(row, col, j) for j in range(pieces)] for row, col in spots]

    arrived(omega.at[pl.ds((r_p * 2 + c) * chunk, chunk)], 24)
    for i in range(8):
        arrived(place(r_d, c, i), 25 + i)
        arrived(place(r_p, 1 - c, i), 33 + i)
        arrived(place(r_d, 1 - c, i), 41 + i)
    loads[2].wait()
    loads[0].wait()

    group = 2
    products = []
    for t in range(count):
        acc = jnp.zeros((128, width), F32)
        for b in range(0, column_ref.shape[1], group):
            chosen = jnp.concatenate([omega[column_ref[t, b + g]] for g in range(group)], axis=0)
            acc = acc + jnp.dot(
                child[t, :, 128 * b : 128 * (b + group)], chosen, preferred_element_type=F32
            )
        products.append(acc)

    def pack(ref, tiles):
        codes = [code_of(tile) for tile in tiles]
        ref[:head, :] = jnp.concatenate(codes, axis=0).astype(jnp.int32).astype(jnp.int16)
        for t, tile in enumerate(tiles):
            at = head + 128 * t
            ref[at : at + 128, :] = coded(tile, codes[t])

    def unpack(ref, t):
        at = head + 128 * t
        return decoded(ref[at : at + 128, :], step_of(ref[:head, :])[8 * t : 8 * t + 8])

    for h in range(2):
        pack(held.at[h, 0, f], [p[:, h * half : (h + 1) * half] for p in products])
        launch(h)

    loads[1].wait()

    @pl.loop(0, slab_rows // 128)
    def _(i):
        rows = pl.ds(pl.multiple_of(i * 128, 128), 128)
        part[rows, :] = jnp.dot(
            slab[rows, :],
            omega[pl.ds(c * (slab_cols // 128), slab_cols // 128)].reshape(slab_cols, width),
            preferred_element_type=F32,
        )

    sums[none] = jnp.zeros((128, half), F32)

    def accumulate(h):
        for n, (side, s, t) in enumerate(sources):
            sums[n] = unpack(held.at[h, side, s], t) + sums[before[n]]

    def block(h, n, j):
        row, col = spots[n]
        total = sums[lasts[n][j]]
        if n >= 2:
            at = pl.multiple_of(col * own_rows + j * 128, 128)
            total = total + part[pl.ds(at, 128), h * half : (h + 1) * half]
        return total

    def hop(h, n):
        target = (to_d, to_x, to_y)[n]
        return rcopy(blocks.at[h, n], got.at[h, n], es.at[h, n], er.at[h, n], target)

    def spread(h):
        for n in range(3):
            pack(blocks.at[h, n], [block(h, n, j) for j in range(pieces)])
            hop(h, n).start()
        for j in range(pieces):
            sampled_ref[128 * j : 128 * (j + 1), h * half : (h + 1) * half] = block(h, 3, j)

    def finish(h):
        for n in range(3):
            hop(h, n).wait_recv()
        for j in range(pieces):
            total = sampled_ref[128 * j : 128 * (j + 1), h * half : (h + 1) * half]
            for n in range(3):
                total = total + unpack(got.at[h, n], j)
            sampled_ref[128 * j : 128 * (j + 1), h * half : (h + 1) * half] = total

    for d in range(1, fronts):
        relay(0, d)
        if d < fronts - 1:
            relay(1, d)
    paired(0)
    accumulate(0)
    spread(0)
    relay(1, fronts - 1)
    paired(1)
    accumulate(1)
    spread(1)
    finish(0)
    finish(1)
    lane = lax.broadcasted_iota(jnp.int32, (own_rows, half), 1)
    masked = []
    for h in range(2):
        total = sampled_ref[:, h * half : (h + 1) * half]
        masked.append(jnp.where(lane + h * half < rank_ref[0], total, 0.0))
    for n, (i, j) in enumerate(((0, 0), (1, 0), (1, 1))):
        gram_own[n] = lax.dot_general(
            masked[i],
            masked[j],
            (((0,), (0,)), ((), ())),
            precision=HI,
            preferred_element_type=F32,
        )
    g = rcopy(gram_own, gram_got, es.at[0, 3], er.at[0, 3], to_y)
    g.start()
    for cp in sent:
        cp.wait_send()
    for ch in range(3):
        drained(ch)
    for h in range(2):
        for n in range(3):
            hop(h, n).wait_send()
    g.wait()
    rank = jnp.full((3, 8, half), rank_ref[0].astype(F32), F32)
    gram_ref[:, half : half + 8, :] = rank
    gram_ref[:, :half, :] = gram_own[...] + gram_got[...]


def sampled_and_gram(
    fronts, slab, samples, child_tiles, parent_front, parent_tile, column_tiles, ranks
):
    width = samples.shape[1]
    half = width // 2
    count = child_tiles.shape[0]
    rows = slab.shape[0] // 2
    hbm = pl.BlockSpec(memory_space=pl.ANY)
    vmem = pl.BlockSpec(memory_space=pltpu.VMEM)
    dma = lambda *n: pltpu.SemaphoreType.DMA(n)
    parent_front, ranks = parent_front.reshape(-1), ranks.reshape(-1)
    return pl.pallas_call(
        functools.partial(sample_kernel, fronts),
        out_shape=(
            jax.ShapeDtypeStruct((rows, width), F32),
            jax.ShapeDtypeStruct((3, half + 8, half), F32),
        ),
        in_specs=[hbm] * 7,
        out_specs=(vmem, vmem),
        scratch_shapes=[
            pltpu.SMEM(parent_tile.shape, jnp.int32),
            pltpu.SMEM(parent_front.shape, jnp.int32),
            pltpu.SMEM(column_tiles.shape, jnp.int32),
            pltpu.SMEM(ranks.shape, jnp.int32),
            pltpu.VMEM((samples.shape[0] // 128 * 8, 128, width), samples.dtype),
            pltpu.VMEM(slab.shape, slab.dtype),
            pltpu.VMEM(child_tiles.shape, child_tiles.dtype),
            pltpu.VMEM((2, fronts, 8, 128), jnp.int32),
            pltpu.SMEM((2, fronts, 8, 128), jnp.int32),
            pltpu.VMEM((2, 2, fronts, 136 * count, half), jnp.int16),
            pltpu.VMEM((2 * fronts * count + 1, 128, half), F32),
            pltpu.VMEM((slab.shape[0], width), F32),
            pltpu.VMEM((2, 3, 8 * count + rows, half), jnp.int16),
            pltpu.VMEM((2, 3, 8 * count + rows, half), jnp.int16),
            pltpu.VMEM((3, half, half), F32),
            pltpu.VMEM((3, half, half), F32),
            dma(8),
            dma(49),
            dma(49),
            dma(3, fronts),
            dma(3, fronts),
            dma(3, fronts),
            dma(3, fronts),
            dma(3, fronts),
            dma(2, 4),
            dma(2, 4),
        ],
        compiler_params=pltpu.CompilerParams(
            collective_id=0, has_side_effects=True, vmem_limit_bytes=67043328
        ),
        name="sampled_and_gram",
    )(
        parent_tile,
        parent_front,
        column_tiles,
        ranks,
        slab,
        samples.reshape(-1, 128, width),
        child_tiles,
    )


def sampled_and_gram_any(
    slab, samples, child_tiles, parent_front, parent_tile, column_tiles, ranks
):
    width = samples.shape[1]
    half = width // 2
    col_width = slab.shape[1]
    omega = lax.all_gather(samples, ("row", "col"), axis=0, tiled=True)
    own = lax.dynamic_slice_in_dim(omega, lax.axis_index("col") * col_width, col_width, 0)
    direct = lax.psum_scatter(
        jnp.dot(slab, own, preferred_element_type=F32), "col", scatter_dimension=0, tiled=True
    )
    count = child_tiles.shape[0]
    blocks = child_tiles.shape[2] // 128
    chosen = omega.reshape(-1, 128, width)[column_tiles]
    pieces = child_tiles.reshape(count, 128, blocks, 128)
    product = jnp.einsum("trkc,tkcs->trs", pieces, chosen, preferred_element_type=F32)
    row_tiles = slab.shape[0] * lax.axis_size("row") // 128
    label = (parent_front[:, 0] * row_tiles + parent_tile).astype(F32)
    product = lax.all_gather(product, "front", axis=0, tiled=True)
    label = lax.all_gather(label, "front", axis=0, tiled=True)
    wanted = (lax.axis_index("front") * row_tiles + jnp.arange(row_tiles)).astype(F32)
    spread = (label[:, None] == wanted[None, :]).astype(F32)
    rows_full = jnp.einsum("qj,qrs->jrs", spread, product, precision=HI)
    rows_full = rows_full.reshape(row_tiles * 128, width)
    extended = lax.psum_scatter(rows_full, ("row", "col"), scatter_dimension=0, tiled=True)
    sampled = direct + extended
    masked = jnp.where(jnp.arange(width)[None, :] < ranks[0, 0], sampled, 0.0)
    gram = lax.psum(jnp.dot(masked.T, masked, precision=HI), "col")
    gram = jnp.stack([gram[:half, :half], gram[half:, :half], gram[half:, half:]])
    rank = jnp.broadcast_to(ranks.astype(F32)[:, :, None], (3, 8, half))
    return sampled, jnp.concatenate([gram, rank], axis=1)


def on_device(
    sizes, front_slab, samples, child_tiles, parent_front, parent_tile, column_tiles, ranks
):
    args = (samples, child_tiles, parent_front, parent_tile, column_tiles, ranks)
    if sizes["row"] == 4 and sizes["col"] == 2 and sizes["front"] % 2 == 0:
        sampled, gram = sampled_and_gram(sizes["front"], front_slab[0], *args)
    else:
        sampled, gram = sampled_and_gram_any(front_slab[0], *args)
    sampled, basis = leaf_bases(sampled, gram)
    return (sampled[None], basis[None])


def solution(mesh):
    in_specs = (
        P("front", "row", "col"),
        P(("row", "col"), None),
        P(("front", "row", "col"), None, None),
        P(("front", "row", "col"), None),
        P(("front", "row", "col")),
        P(("front", "row", "col"), None),
        P("front", "row"),
    )
    out_specs = (P("front", ("row", "col"), None), P("front", ("row", "col"), None))
    return jax.shard_map(
        functools.partial(on_device, dict(mesh.shape)),
        mesh=mesh,
        in_specs=in_specs,
        out_specs=out_specs,
        check_vma=False,
    )
```

```python
import functools

import jax
import jax.numpy as jnp
from jax import lax
from jax.experimental import pallas as pl
from jax.experimental.pallas import tpu as pltpu
from jax.sharding import PartitionSpec as P

F32 = jnp.float32
HI = lax.Precision.HIGHEST
LOGICAL = pl.DeviceIdType.MESH


def dot_nt(a, b):
    return lax.dot_general(a, b, (((1,), (1,)), ((), ())), precision=HI, preferred_element_type=F32)


def inverse_factor(a):
    n = a.shape[0]
    tiles = n // 8
    w = [a[8 * t : 8 * t + 8, :] for t in range(tiles)]
    lane = lax.broadcasted_iota(jnp.int32, (8, n), 1)
    sub = lax.broadcasted_iota(jnp.int32, (8, n), 0)
    rows = []
    for t in range(tiles):
        base = 8 * t
        inside = (lane >= base) & (lane < base + 8)
        cols = [jnp.broadcast_to(w[t][:, base + k : base + k + 1], (8, n)) for k in range(8)]
        v = jnp.where(inside, jnp.where(lane - base == sub, 1.0, 0.0), w[t])
        done, pivots = v, cols[0]
        for k in range(8):
            here = sub == k
            pivot = jnp.broadcast_to(cols[k][k : k + 1, :], (8, n))
            inv = 1.0 / pivot
            done = jnp.where(here, v, done)
            pivots = jnp.where(here, pivot, pivots)
            step = jnp.broadcast_to(v[k : k + 1, :], (8, n)) * inv
            v = jnp.where(here, step, v - cols[k] * step)
            for m in range(k + 1, 8):
                step = jnp.broadcast_to(cols[m][k : k + 1, :], (8, n)) * inv
                cols[m] = jnp.where(here, step, cols[m] - cols[k] * step)
        rows.append(jnp.where(lane < base + 8, done, 0.0) * lax.rsqrt(pivots))
        vk = [jnp.broadcast_to(v[k : k + 1, :], (8, n)) for k in range(8)]
        for u in range(t + 1, tiles):
            x = jnp.where(inside, 0.0, w[u])
            terms = [
                jnp.broadcast_to(w[u][:, base + k : base + k + 1], (8, n)) * vk[k] for k in range(8)
            ]
            low = (terms[0] + terms[1]) + (terms[2] + terms[3])
            high = (terms[4] + terms[5]) + (terms[6] + terms[7])
            w[u] = x - (low + high)
    return jnp.concatenate(rows, axis=0)


def basis_kernel(sampled_ref, gram_ref, out_ref, basis_ref):
    half = gram_ref.shape[2]
    rank = gram_ref[0, half : half + 1, :]
    sampled = sampled_ref[...]
    out_ref[...] = sampled
    rows = sampled.shape[0]
    lane = lax.broadcasted_iota(jnp.int32, (rows, half), 1).astype(F32)
    first = jnp.where(lane < rank, sampled[:, :half], 0.0)
    second = jnp.where(lane + half < rank, sampled[:, half:], 0.0)
    r = lax.broadcasted_iota(jnp.int32, (half, half), 0)
    c = lax.broadcasted_iota(jnp.int32, (half, half), 1)
    lane = c.astype(F32)
    a = gram_ref[0, :half, :] + jnp.where((r == c) & (lane >= rank), 1.0, 0.0)
    inv1 = inverse_factor(a)
    low = dot_nt(gram_ref[1, :half, :], inv1)
    a = gram_ref[2, :half, :] + jnp.where((r == c) & (lane + half >= rank), 1.0, 0.0)
    a = a - dot_nt(low, low)
    inv2 = inverse_factor(a)
    basis = dot_nt(first, inv1)
    basis_ref[:, :half] = basis
    basis_ref[:, half:] = dot_nt(second - dot_nt(basis, low), inv2)


def leaf_bases(sampled, gram):
    vmem = pl.BlockSpec(memory_space=pltpu.VMEM)
    return pl.pallas_call(
        basis_kernel,
        out_shape=(jax.ShapeDtypeStruct(sampled.shape, F32),) * 2,
        in_specs=[vmem, vmem],
        out_specs=(vmem, vmem),
        name="leaf_bases",
    )(sampled, gram)


LEVELS = 32767.0


def widened(code):
    return code.astype(jnp.int32).astype(F32)


def step_of(code):
    return jnp.exp2(widened(code) * (1.0 / 256.0)) * (1.0 / LEVELS)


def code_of(block):
    peak = jnp.max(jnp.max(jnp.abs(block), axis=0, keepdims=True), axis=1, keepdims=True)
    peak = jnp.broadcast_to(jnp.maximum(peak, 1e-30), (8, 128))
    return jnp.ceil(jnp.log2(peak) * 256.0) + 2.0


def coded(block, code):
    rows, lanes = block.shape
    scale = jnp.exp2(code * (-1.0 / 256.0)) * LEVELS
    scaled = (block.reshape(rows // 8, 8, lanes) * scale[None]).reshape(rows, lanes)
    return jnp.round(scaled).astype(jnp.int32).astype(jnp.int16)


def decoded(words, step):
    rows, lanes = words.shape
    values = widened(words).reshape(rows // 8, 8, lanes) * step[None]
    return values.reshape(rows, lanes)


def sample_kernel(
    tile_hbm,
    front_hbm,
    column_hbm,
    rank_hbm,
    slab_ref,
    samples_ref,
    child_ref,
    sampled_ref,
    basis_ref,
    tile_ref,
    front_ref,
    column_ref,
    rank_ref,
    omega_low,
    omega_high,
    slab,
    child,
    labels,
    label_ref,
    held,
    sums,
    part,
    blocks,
    got,
    gram_own,
    gram_got,
    copy_sem,
    gs,
    gr,
    zs,
    zr,
    es,
    er,
):
    f, r, c = lax.axis_index("front"), lax.axis_index("row"), lax.axis_index("col")
    omega = (omega_low, omega_high)
    x, core = r // 2, r % 2
    width = samples_ref.shape[2]
    half = width // 2
    chunk = samples_ref.shape[0]
    piece = chunk // 8
    odd = f % 2
    count = child_ref.shape[0]
    slab_rows, slab_cols = slab_ref.shape
    own_rows = slab_rows // 2
    pieces = own_rows // 128
    row_tiles = slab_rows * 4 // 128
    head = 8 * count
    r_x = (1 - x) * 2 + core
    r_p = x * 2 + (1 - core)
    r_d = (1 - x) * 2 + (1 - core)
    to_x, to_y, to_p, to_d = (f, r_x, c), (f, r, 1 - c), (f, r_p, c), (f, r_x, 1 - c)
    right, left = (f + 1, r, c), (f - 1, r, c)
    to_z, to_two = (f + 1 - 2 * odd, r, c), ((f + 2) % 4, r, c)
    base = (r * 2 + c) * chunk

    loads = [
        pltpu.make_async_copy(child_ref, child, copy_sem.at[0]),
        pltpu.make_async_copy(slab_ref, slab, copy_sem.at[1]),
    ]
    own_loads = [
        pltpu.make_async_copy(
            samples_ref.at[:, :, pl.ds(h * half, half)],
            omega[h].at[pl.ds(base, chunk)],
            copy_sem.at[8 + h],
        )
        for h in range(2)
    ]
    small = [
        pltpu.make_async_copy(src, dst, copy_sem.at[3 + n])
        for n, (src, dst) in enumerate(
            (
                (tile_hbm, tile_ref),
                (front_hbm, front_ref),
                (column_hbm, column_ref),
                (rank_hbm, rank_ref),
            )
        )
    ]
    for cp in own_loads + small:
        cp.start()
    loads[0].start()
    loads[1].start()

    barrier = pltpu.get_barrier_semaphore()
    for target in (to_x, to_y, to_p, to_d, to_two):
        pl.semaphore_signal(barrier, inc=1, device_id=target, device_id_type=LOGICAL)

    @pl.when(f < 3)
    def _():
        pl.semaphore_signal(barrier, inc=1, device_id=right, device_id_type=LOGICAL)

    @pl.when(f > 0)
    def _():
        pl.semaphore_signal(barrier, inc=1, device_id=left, device_id_type=LOGICAL)

    pl.semaphore_wait(barrier, 5 + jnp.minimum(f, 1) + jnp.minimum(3 - f, 1))

    def rcopy(src, dst, send, recv, target):
        return pltpu.make_async_remote_copy(
            src_ref=src,
            dst_ref=dst,
            send_sem=send,
            recv_sem=recv,
            device_id=target,
            device_id_type=LOGICAL,
        )

    def place(h, row, col, i, n=1):
        start = (row * 2 + col) * chunk + (i + odd * (8 - n - 2 * i)) * piece
        return omega[h].at[pl.ds(start, n * piece)]

    via_z = (3, 1)

    def send(h, ref, n, target):
        rcopy(ref, ref, gs.at[h], gr.at[h, n], target).start()

    def arrived(h, ref, n):
        rcopy(ref, ref, gs.at[h], gr.at[h, n], to_p).wait_recv()

    def all_arrived(h, amount, n):
        arrived(h, omega[h].at[pl.ds(0, amount * piece)], n)

    def pair_up(h, row, col, i, n=1):
        send(h, place(h, row, col, i, n), 12, to_p)

    def gather_own(h):
        own_loads[h].wait()
        for i in range(8 - via_z[h]):
            send(h, place(h, r, c, i), i if i < 4 else 8, to_x)
            send(h, place(h, r, c, 7 - i), 4 + i if i < 4 else 8, to_y)
        pair_up(h, r, c, 0, 8)

    def gather_near(h, i):
        ref = place(h, r_x, c, i)
        arrived(h, ref, i)
        if i < via_z[h]:
            send(h, ref, 9, to_z)
        send(h, ref, 10 + i // 2, to_y)
        pair_up(h, r_x, c, i)
        ref = place(h, r, 1 - c, 7 - i)
        arrived(h, ref, 4 + i)
        if i < via_z[h]:
            send(h, ref, 9, to_z)
        send(h, ref, 10 + i // 2, to_x)
        pair_up(h, r, 1 - c, 7 - i)

    def gather_rest(h):
        n = 4 - via_z[h]
        all_arrived(h, 2 * n, 8)
        pair_up(h, r_x, c, 4, n)
        pair_up(h, r, 1 - c, 4 - n, n)

    def gather_z(h):
        n = via_z[h]
        all_arrived(h, 2 * n, 9)
        pair_up(h, r_x, c, 8 - n, n)
        pair_up(h, r, 1 - c, 0, n)

    def gather_far(h, g):
        all_arrived(h, 4, 10 + g)
        pair_up(h, r_x, 1 - c, 2 * g, 2)
        pair_up(h, r_x, 1 - c, 6 - 2 * g, 2)

    def gather_pair(h):
        all_arrived(h, 32, 12)

    def gather_sent():
        for h in range(2):
            every = omega[h].at[pl.ds(0, 56 * piece)]
            rcopy(every, every, gs.at[h], gr.at[h, 0], to_p).wait_send()

    def view(ch, side, src, n=1):
        if ch == 2:
            return labels.at[side, pl.ds(src, n)]
        return held.at[ch, side, pl.ds(src, n)]

    def along(src, ch, n, target):
        ref = view(ch, 0, src)
        return rcopy(ref, ref, zs.at[ch // 2], zr.at[ch, n], target)

    def across(ch, src, n=1):
        rcopy(view(ch, 0, src, n), view(ch, 1, src, n), zs.at[ch // 2], zr.at[ch, 2], to_p).start()

    def launch(ch):
        @pl.when((f == 0) | (f == 3))
        def _():
            along(f, ch, 1, to_two).start()

        @pl.when((f == 1) | (f == 2))
        def _():
            along(f, ch, 0, to_two).start()

        @pl.when(f < 3)
        def _():
            along(f, ch, 0, right).start()

        @pl.when(f > 0)
        def _():
            along(f, ch, 0, left).start()

        across(ch, f)

    def relay(ch):
        @pl.when(f == 1)
        def _():
            along(3, ch, 1, left).wait_recv()
            along(3, ch, 0, left).start()
            across(ch, 3)

        @pl.when(f == 2)
        def _():
            along(0, ch, 1, right).wait_recv()
            along(0, ch, 0, right).start()
            across(ch, 0)

    def came(ch, amount):
        ref = view(ch, 0, 0, amount)
        rcopy(ref, ref, zs.at[ch // 2], zr.at[ch, 0], to_p).wait_recv()

    def collect(ch):
        @pl.when((f == 0) | (f == 3))
        def _():
            came(ch, 3)
            across(ch, 1 - f // 3, 3)

        @pl.when((f == 1) | (f == 2))
        def _():
            came(ch, 2)
            across(ch, f - 1)
            across(ch, f + 1)

    def paired(ch):
        ref = view(ch, 1, 0, 4)
        rcopy(ref, ref, zs.at[ch // 2], zr.at[ch, 2], to_p).wait_recv()

    def drained():
        def wait(buffer, n, sem):
            ref = buffer.at[..., pl.ds(0, n), :, :]
            rcopy(ref, ref, zs.at[sem], zr.at[0, 0], to_p).wait_send()

        @pl.when((f == 0) | (f == 3))
        def _():
            wait(held, 3, 0)
            wait(labels, 3, 1)

        @pl.when((f == 1) | (f == 2))
        def _():
            wait(held, 4, 0)
            wait(labels, 4, 1)

    gather_own(0)
    for cp in small:
        cp.wait()
    at_row = lax.broadcasted_iota(jnp.int32, (8, 128), 0)
    own_labels = jnp.zeros((8, 128), jnp.int32)
    for t in range(count):
        label = front_ref[t] * row_tiles + tile_ref[t]
        own_labels = jnp.where(at_row == t, label, own_labels)
    labels[0, f] = own_labels
    launch(2)
    for i in range(4):
        gather_near(0, i)
    gather_own(1)
    gather_rest(0)
    relay(2)
    gather_far(0, 0)
    gather_z(0)
    collect(2)
    gather_far(0, 1)
    gather_pair(0)
    loads[0].wait()

    def product(h, t):
        acc = jnp.zeros((128, half), F32)
        for b in range(0, column_ref.shape[1], 2):
            chosen = jnp.concatenate([omega[h][column_ref[t, b + g]] for g in range(2)], axis=0)
            acc = acc + jnp.dot(
                child[t, :, 128 * b : 128 * (b + 2)], chosen, preferred_element_type=F32
            )
        return acc

    def pack(ref, tiles):
        codes = [code_of(tile) for tile in tiles]
        ref[:head, :] = jnp.concatenate(codes, axis=0).astype(jnp.int32).astype(jnp.int16)
        for t, tile in enumerate(tiles):
            at = head + 128 * t
            ref[at : at + 128, :] = coded(tile, codes[t])

    def unpack(ref, t):
        at = head + 128 * t
        return decoded(ref[at : at + 128, :], step_of(ref[:head, :])[8 * t : 8 * t + 8])

    def direct(h):
        @pl.loop(0, slab_rows // 128)
        def _(i):
            rows = pl.ds(pl.multiple_of(i * 128, 128), 128)
            part[h, rows, :] = jnp.dot(
                slab[rows, :],
                omega[h][pl.ds(c * (slab_cols // 128), slab_cols // 128)].reshape(slab_cols, half),
                preferred_element_type=F32,
            )

    pack(held.at[0, 0, f], [product(0, t) for t in range(count)])
    launch(0)
    for i in range(4):
        gather_near(1, i)
    paired(2)
    to_smem = pltpu.make_async_copy(labels, label_ref, copy_sem.at[7])
    to_smem.start()
    loads[1].wait()
    direct(0)
    to_smem.wait()

    sources = [(side, s, t) for s in range(4) for side in range(2) for t in range(count)]
    none = len(sources)
    known = [label_ref[side, s, t, 0] for side, s, t in sources]
    before = []
    for n, label in enumerate(known):
        prev = jnp.int32(none)
        for m in range(n):
            prev = jnp.where(known[m] == label, m, prev)
        before.append(prev)

    def last_of(row, col, j):
        wanted = f * row_tiles + (row * 2 + col) * pieces + j
        last = jnp.int32(none)
        for n, label in enumerate(known):
            last = jnp.where(label == wanted, n, last)
        return last

    spots = [(r_x, 1 - c), (r_x, c), (r, 1 - c), (r, c)]
    lasts = [[last_of(row, col, j) for j in range(pieces)] for row, col in spots]

    gather_rest(1)
    gather_z(1)
    gather_far(1, 0)
    relay(0)
    gather_far(1, 1)
    gather_pair(1)
    pack(held.at[1, 0, f], [product(1, t) for t in range(count)])
    launch(1)
    direct(1)
    sums[none] = jnp.zeros((128, half), F32)

    def accumulate(h):
        for n, (side, s, t) in enumerate(sources):
            sums[n] = unpack(held.at[h, side, s], t) + sums[before[n]]

    def block(h, n, j):
        row, col = spots[n]
        total = sums[lasts[n][j]]
        if n >= 2:
            at = pl.multiple_of(col * own_rows + j * 128, 128)
            total = total + part[h, pl.ds(at, 128), :]
        return total

    def hop(h, n):
        target = (to_d, to_x, to_y)[n]
        return rcopy(blocks.at[h, n], got.at[h, n], es.at[0], er.at[h], target)

    def spread(h):
        for n in range(3):
            pack(blocks.at[h, n], [block(h, n, j) for j in range(pieces)])
            hop(h, n).start()
        for j in range(pieces):
            sampled_ref[128 * j : 128 * (j + 1), h * half : (h + 1) * half] = block(h, 3, j)

    def finish(h):
        rcopy(got.at[h], got.at[h], es.at[0], er.at[h], to_p).wait_recv()
        for j in range(pieces):
            total = sampled_ref[128 * j : 128 * (j + 1), h * half : (h + 1) * half]
            for n in range(3):
                total = total + unpack(got.at[h, n], j)
            sampled_ref[128 * j : 128 * (j + 1), h * half : (h + 1) * half] = total

    def masked(h):
        lane = lax.broadcasted_iota(jnp.int32, (own_rows, half), 1) + h * half
        return jnp.where(lane < rank_ref[0], sampled_ref[:, h * half : (h + 1) * half], 0.0)

    def gram_hop(n):
        return rcopy(gram_own.at[n], gram_got.at[n], es.at[1], er.at[2 + n], to_y)

    def gram_send(n, i, j):
        gram_own[n] = lax.dot_general(
            masked(i),
            masked(j),
            (((0,), (0,)), ((), ())),
            precision=HI,
            preferred_element_type=F32,
        )
        gram_hop(n).start()

    def gram_total(n):
        gram_hop(n).wait_recv()
        total = gram_own[n] + gram_got[n]
        if n == 1:
            return total
        row = lax.broadcasted_iota(jnp.int32, (half, half), 0)
        lane = lax.broadcasted_iota(jnp.int32, (half, half), 1)
        beyond = (row == lane) & (lane + (n // 2) * half >= rank_ref[0])
        return total + jnp.where(beyond, 1.0, 0.0)

    collect(0)
    paired(0)
    accumulate(0)
    spread(0)
    relay(1)
    collect(1)
    paired(1)
    accumulate(1)
    spread(1)
    finish(0)
    gram_send(0, 0, 0)
    finish(1)
    gram_send(1, 1, 0)
    gram_send(2, 1, 1)
    gram = gram_total(0)
    inv1 = inverse_factor(gram)
    low = dot_nt(gram_total(1), inv1)
    inv2 = inverse_factor(gram_total(2) - dot_nt(low, low))
    basis = dot_nt(masked(0), inv1)
    basis_ref[:, :half] = basis
    basis_ref[:, half:] = dot_nt(masked(1) - dot_nt(basis, low), inv2)
    gather_sent()
    drained()
    rcopy(blocks, got, es.at[0], er.at[0], to_p).wait_send()
    rcopy(gram_own, gram_got, es.at[1], er.at[0], to_p).wait_send()


def sampled_and_bases(
    slab, samples, child_tiles, parent_front, parent_tile, column_tiles, ranks
):
    width = samples.shape[1]
    half = width // 2
    count = child_tiles.shape[0]
    rows = slab.shape[0] // 2
    hbm = pl.BlockSpec(memory_space=pl.ANY)
    vmem = pl.BlockSpec(memory_space=pltpu.VMEM)
    dma = lambda *n: pltpu.SemaphoreType.DMA(n)
    parent_front, ranks = parent_front.reshape(-1), ranks.reshape(-1)
    return pl.pallas_call(
        sample_kernel,
        out_shape=(jax.ShapeDtypeStruct((rows, width), F32),) * 2,
        in_specs=[hbm] * 7,
        out_specs=(vmem, vmem),
        scratch_shapes=[
            pltpu.SMEM(parent_tile.shape, jnp.int32),
            pltpu.SMEM(parent_front.shape, jnp.int32),
            pltpu.SMEM(column_tiles.shape, jnp.int32),
            pltpu.SMEM(ranks.shape, jnp.int32),
            pltpu.VMEM((samples.shape[0] // 128 * 8, 128, half), samples.dtype),
            pltpu.VMEM((samples.shape[0] // 128 * 8, 128, half), samples.dtype),
            pltpu.VMEM(slab.shape, slab.dtype),
            pltpu.VMEM(child_tiles.shape, child_tiles.dtype),
            pltpu.VMEM((2, 4, 8, 128), jnp.int32),
            pltpu.SMEM((2, 4, 8, 128), jnp.int32),
            pltpu.VMEM((2, 2, 4, 136 * count, half), jnp.int16),
            pltpu.VMEM((8 * count + 1, 128, half), F32),
            pltpu.VMEM((2, slab.shape[0], half), F32),
            pltpu.VMEM((2, 3, 8 * count + rows, half), jnp.int16),
            pltpu.VMEM((2, 3, 8 * count + rows, half), jnp.int16),
            pltpu.VMEM((3, half, half), F32),
            pltpu.VMEM((3, half, half), F32),
            dma(10),
            dma(2),
            dma(2, 13),
            dma(2),
            dma(3, 3),
            dma(2),
            dma(5),
        ],
        compiler_params=pltpu.CompilerParams(
            collective_id=0, has_side_effects=True, vmem_limit_bytes=48 * 1024 * 1024
        ),
        name="sampled_and_bases",
    )(
        *[
            a if a is ranks else pltpu.with_memory_space_constraint(a, pltpu.HBM)
            for a in (
                parent_tile,
                parent_front,
                column_tiles,
                ranks,
                slab,
                samples.reshape(-1, 128, width),
                child_tiles,
            )
        ]
    )


def sampled_and_gram_any(
    slab, samples, child_tiles, parent_front, parent_tile, column_tiles, ranks
):
    width = samples.shape[1]
    half = width // 2
    col_width = slab.shape[1]
    omega = lax.all_gather(samples, ("row", "col"), axis=0, tiled=True)
    own = lax.dynamic_slice_in_dim(omega, lax.axis_index("col") * col_width, col_width, 0)
    direct = lax.psum_scatter(
        jnp.dot(slab, own, preferred_element_type=F32), "col", scatter_dimension=0, tiled=True
    )
    count = child_tiles.shape[0]
    blocks = child_tiles.shape[2] // 128
    chosen = omega.reshape(-1, 128, width)[column_tiles]
    pieces = child_tiles.reshape(count, 128, blocks, 128)
    product = jnp.einsum("trkc,tkcs->trs", pieces, chosen, preferred_element_type=F32)
    row_tiles = slab.shape[0] * lax.axis_size("row") // 128
    label = (parent_front[:, 0] * row_tiles + parent_tile).astype(F32)
    product = lax.all_gather(product, "front", axis=0, tiled=True)
    label = lax.all_gather(label, "front", axis=0, tiled=True)
    wanted = (lax.axis_index("front") * row_tiles + jnp.arange(row_tiles)).astype(F32)
    spread = (label[:, None] == wanted[None, :]).astype(F32)
    rows_full = jnp.einsum("qj,qrs->jrs", spread, product, precision=HI)
    rows_full = rows_full.reshape(row_tiles * 128, width)
    extended = lax.psum_scatter(rows_full, ("row", "col"), scatter_dimension=0, tiled=True)
    sampled = direct + extended
    masked = jnp.where(jnp.arange(width)[None, :] < ranks[0, 0], sampled, 0.0)
    gram = lax.psum(jnp.dot(masked.T, masked, precision=HI), "col")
    gram = jnp.stack([gram[:half, :half], gram[half:, :half], gram[half:, half:]])
    rank = jnp.broadcast_to(ranks.astype(F32)[:, :, None], (3, 8, half))
    return sampled, jnp.concatenate([gram, rank], axis=1)


def on_device(
    sizes, front_slab, samples, child_tiles, parent_front, parent_tile, column_tiles, ranks
):
    args = (samples, child_tiles, parent_front, parent_tile, column_tiles, ranks)
    tiles, count = samples.shape[0] // 128, child_tiles.shape[0]
    near = sizes["row"] == 4 and sizes["col"] == 2 and sizes["front"] == 4
    if near and tiles % 8 == 0 and count == 2 and front_slab.shape[1] == 512:
        sampled, basis = sampled_and_bases(front_slab[0], *args)
    else:
        sampled, gram = sampled_and_gram_any(front_slab[0], *args)
        sampled, basis = leaf_bases(sampled, gram)
    return (sampled[None], basis[None])


def solution(mesh):
    in_specs = (
        P("front", "row", "col"),
        P(("row", "col"), None),
        P(("front", "row", "col"), None, None),
        P(("front", "row", "col"), None),
        P(("front", "row", "col")),
        P(("front", "row", "col"), None),
        P("front", "row"),
    )
    out_specs = (P("front", ("row", "col"), None), P("front", ("row", "col"), None))
    return jax.shard_map(
        functools.partial(on_device, dict(mesh.shape)),
        mesh=mesh,
        in_specs=in_specs,
        out_specs=out_specs,
        check_vma=False,
    )
```

```python
import functools

import jax
import jax.numpy as jnp
from jax import lax
from jax.experimental import pallas as pl
from jax.experimental.pallas import tpu as pltpu
from jax.sharding import PartitionSpec as P

F32 = jnp.float32
HI = lax.Precision.HIGHEST
LOGICAL = pl.DeviceIdType.MESH


def dot_nt(a, b):
    return lax.dot_general(a, b, (((1,), (1,)), ((), ())), precision=HI, preferred_element_type=F32)


def row_of(x, k):
    return jnp.broadcast_to(x[k : k + 1, :], (8, x.shape[1]))
def inverse_factor(a, B=2):
    n = a.shape[0]
    r = lax.broadcasted_iota(jnp.int32, (n, n), 0)
    l = lax.broadcasted_iota(jnp.int32, (n, n), 1)
    diagonal = jnp.where(r == l, a, 0.0)
    across = lax.rsqrt(jnp.sum(diagonal, axis=0, keepdims=True))
    down = lax.rsqrt(jnp.sum(diagonal, axis=1, keepdims=True))
    a = a * across * down
    w = [a[8 * t : 8 * t + 8, :] for t in range(n // 8)]
    lane = lax.broadcasted_iota(jnp.int32, (8, n), 1)
    sub = lax.broadcasted_iota(jnp.int32, (8, n), 0)
    at = [sub == k for k in range(8)]
    size = 8 * B
    rows = []
    for first in range(0, n // 8, B):
        base = 8 * first
        inside = (lane >= base) & (lane < base + size)
        mine = w[first : first + B]
        cols = [[jnp.broadcast_to(x[:, base + k : base + k + 1], (8, n)) for x in mine] for k in range(size)]
        v = [jnp.where(inside, jnp.where(lane - base - 8 * t == sub, 1.0, 0.0), x) for t, x in enumerate(mine)]
        done = [None] * B
        pivots = [None] * B
        for k in range(0, size, 2):
            t, s = k // 8, k % 8
            left, right = cols[k], cols[k + 1]
            p, q, u = row_of(left[t], s), row_of(right[t], s), row_of(right[t], s + 1)
            det = p * u - q * q
            inv = 1.0 / det
            ratio = 1.0 / p
            v0, v1 = row_of(v[t], s), row_of(v[t], s + 1)
            second = v1 - (q * ratio) * v0
            if s == 0:
                done[t], pivots[t] = v0, p
            else:
                done[t] = jnp.where(at[s], v0, done[t])
                pivots[t] = jnp.where(at[s], p, pivots[t])
            done[t] = jnp.where(at[s + 1], second, done[t])
            pivots[t] = jnp.where(at[s + 1], det * ratio, pivots[t])

            def step(x, x0, x1):
                y0 = u * x0 - q * x1
                y1 = p * x1 - q * x0
                out = [x[i] - (left[i] * y0 + right[i] * y1) * inv for i in range(B)]
                out[t] = jnp.where(at[s], y0 * inv, jnp.where(at[s + 1], y1 * inv, out[t]))
                return out

            v = step(v, v0, v1)
            for m in range(k + 2, size):
                cols[m] = step(cols[m], row_of(cols[m][t], s), row_of(cols[m][t], s + 1))
        for t in range(B):
            rows.append(jnp.where(lane < base + 8 * (t + 1), done[t], 0.0) * lax.rsqrt(pivots[t]) * across)
        vk = [row_of(v[k // 8], k % 8) for k in range(size)]
        for i in range(first + B, n // 8):
            terms = [jnp.broadcast_to(w[i][:, base + k : base + k + 1], (8, n)) * vk[k] for k in range(size)]
            while len(terms) > 1:
                terms = [x + y for x, y in zip(terms[::2], terms[1::2])]
            w[i] = jnp.where(inside, 0.0, w[i]) - terms[0]
    return jnp.concatenate(rows, axis=0)


def basis_kernel(sampled_ref, gram_ref, out_ref, basis_ref):
    half = gram_ref.shape[2]
    rank = gram_ref[0, half : half + 1, :]
    sampled = sampled_ref[...]
    out_ref[...] = sampled
    rows = sampled.shape[0]
    lane = lax.broadcasted_iota(jnp.int32, (rows, half), 1).astype(F32)
    first = jnp.where(lane < rank, sampled[:, :half], 0.0)
    second = jnp.where(lane + half < rank, sampled[:, half:], 0.0)
    r = lax.broadcasted_iota(jnp.int32, (half, half), 0)
    c = lax.broadcasted_iota(jnp.int32, (half, half), 1)
    lane = c.astype(F32)
    a = gram_ref[0, :half, :] + jnp.where((r == c) & (lane >= rank), 1.0, 0.0)
    inv1 = inverse_factor(a)
    low = dot_nt(gram_ref[1, :half, :], inv1)
    a = gram_ref[2, :half, :] + jnp.where((r == c) & (lane + half >= rank), 1.0, 0.0)
    a = a - dot_nt(low, low)
    inv2 = inverse_factor(a)
    basis = dot_nt(first, inv1)
    basis_ref[:, :half] = basis
    basis_ref[:, half:] = dot_nt(second - dot_nt(basis, low), inv2)


def leaf_bases(sampled, gram):
    vmem = pl.BlockSpec(memory_space=pltpu.VMEM)
    return pl.pallas_call(
        basis_kernel,
        out_shape=(jax.ShapeDtypeStruct(sampled.shape, F32),) * 2,
        in_specs=[vmem, vmem],
        out_specs=(vmem, vmem),
        name="leaf_bases",
    )(sampled, gram)


LEVELS = 32767.0


def widened(code):
    return code.astype(jnp.int32).astype(F32)


def step_of(code):
    return jnp.exp2(widened(code) * (1.0 / 256.0)) * (1.0 / LEVELS)


def code_of(block):
    peak = jnp.max(jnp.max(jnp.abs(block), axis=0, keepdims=True), axis=1, keepdims=True)
    peak = jnp.broadcast_to(jnp.maximum(peak, 1e-30), (8, 128))
    return jnp.ceil(jnp.log2(peak) * 256.0) + 2.0


def coded(block, code):
    rows, lanes = block.shape
    scale = jnp.exp2(code * (-1.0 / 256.0)) * LEVELS
    scaled = (block.reshape(rows // 8, 8, lanes) * scale[None]).reshape(rows, lanes)
    return jnp.round(scaled).astype(jnp.int32).astype(jnp.int16)


def decoded(words, step):
    rows, lanes = words.shape
    values = widened(words).reshape(rows // 8, 8, lanes) * step[None]
    return values.reshape(rows, lanes)


def sample_kernel(
    tile_hbm,
    front_hbm,
    column_hbm,
    rank_hbm,
    slab_ref,
    samples_ref,
    child_ref,
    sampled_ref,
    basis_ref,
    tile_ref,
    front_ref,
    column_ref,
    rank_ref,
    omega_low,
    omega_high,
    slab,
    child,
    labels,
    label_ref,
    held,
    sums,
    part,
    blocks,
    got,
    gram_own,
    gram_got,
    copy_sem,
    gs,
    gr,
    zs,
    zr,
    es,
    er,
):
    f, r, c = lax.axis_index("front"), lax.axis_index("row"), lax.axis_index("col")
    omega = (omega_low, omega_high)
    x, core = r // 2, r % 2
    width = samples_ref.shape[2]
    half = width // 2
    chunk = samples_ref.shape[0]
    piece = chunk // 8
    odd = f % 2
    count = child_ref.shape[0]
    slab_rows, slab_cols = slab_ref.shape
    own_rows = slab_rows // 2
    pieces = own_rows // 128
    row_tiles = slab_rows * 4 // 128
    head = 8 * count
    r_x = (1 - x) * 2 + core
    r_p = x * 2 + (1 - core)
    r_d = (1 - x) * 2 + (1 - core)
    to_x, to_y, to_p, to_d = (f, r_x, c), (f, r, 1 - c), (f, r_p, c), (f, r_x, 1 - c)
    right, left = (f + 1, r, c), (f - 1, r, c)
    to_z, to_two = (f + 1 - 2 * odd, r, c), ((f + 2) % 4, r, c)
    base = (r * 2 + c) * chunk

    loads = [
        pltpu.make_async_copy(child_ref, child, copy_sem.at[0]),
        pltpu.make_async_copy(slab_ref, slab, copy_sem.at[1]),
    ]
    own_loads = [
        pltpu.make_async_copy(
            samples_ref.at[:, :, pl.ds(h * half, half)],
            omega[h].at[pl.ds(base, chunk)],
            copy_sem.at[8 + h],
        )
        for h in range(2)
    ]
    small = [
        pltpu.make_async_copy(src, dst, copy_sem.at[3 + n])
        for n, (src, dst) in enumerate(
            (
                (tile_hbm, tile_ref),
                (front_hbm, front_ref),
                (column_hbm, column_ref),
                (rank_hbm, rank_ref),
            )
        )
    ]
    for cp in own_loads + small:
        cp.start()
    loads[0].start()
    loads[1].start()

    barrier = pltpu.get_barrier_semaphore()
    for target in (to_x, to_y, to_p, to_d, to_two):
        pl.semaphore_signal(barrier, inc=1, device_id=target, device_id_type=LOGICAL)

    @pl.when(f < 3)
    def _():
        pl.semaphore_signal(barrier, inc=1, device_id=right, device_id_type=LOGICAL)

    @pl.when(f > 0)
    def _():
        pl.semaphore_signal(barrier, inc=1, device_id=left, device_id_type=LOGICAL)

    pl.semaphore_wait(barrier, 5 + jnp.minimum(f, 1) + jnp.minimum(3 - f, 1))

    def rcopy(src, dst, send, recv, target):
        return pltpu.make_async_remote_copy(
            src_ref=src,
            dst_ref=dst,
            send_sem=send,
            recv_sem=recv,
            device_id=target,
            device_id_type=LOGICAL,
        )

    def place(h, row, col, i, n=1):
        start = (row * 2 + col) * chunk + (i + odd * (8 - n - 2 * i)) * piece
        return omega[h].at[pl.ds(start, n * piece)]

    via_z = (3, 1)

    def send(h, ref, n, target):
        rcopy(ref, ref, gs.at[h], gr.at[h, n], target).start()

    def arrived(h, ref, n):
        rcopy(ref, ref, gs.at[h], gr.at[h, n], to_p).wait_recv()

    def all_arrived(h, amount, n):
        arrived(h, omega[h].at[pl.ds(0, amount * piece)], n)

    def pair_up(h, row, col, i, n=1):
        send(h, place(h, row, col, i, n), 12, to_p)

    def gather_own(h):
        own_loads[h].wait()
        for i in range(8 - via_z[h]):
            send(h, place(h, r, c, i), i if i < 4 else 8, to_x)
            send(h, place(h, r, c, 7 - i), 4 + i if i < 4 else 8, to_y)
        pair_up(h, r, c, 0, 8)

    def gather_near(h, i):
        ref = place(h, r_x, c, i)
        arrived(h, ref, i)
        if i < via_z[h]:
            send(h, ref, 9, to_z)
        send(h, ref, 10 + i // 2, to_y)
        pair_up(h, r_x, c, i)
        ref = place(h, r, 1 - c, 7 - i)
        arrived(h, ref, 4 + i)
        if i < via_z[h]:
            send(h, ref, 9, to_z)
        send(h, ref, 10 + i // 2, to_x)
        pair_up(h, r, 1 - c, 7 - i)

    def gather_rest(h):
        n = 4 - via_z[h]
        all_arrived(h, 2 * n, 8)
        pair_up(h, r_x, c, 4, n)
        pair_up(h, r, 1 - c, 4 - n, n)

    def gather_z(h):
        n = via_z[h]
        all_arrived(h, 2 * n, 9)
        pair_up(h, r_x, c, 8 - n, n)
        pair_up(h, r, 1 - c, 0, n)

    def gather_far(h, g):
        all_arrived(h, 4, 10 + g)
        pair_up(h, r_x, 1 - c, 2 * g, 2)
        pair_up(h, r_x, 1 - c, 6 - 2 * g, 2)

    def gather_pair(h):
        all_arrived(h, 32, 12)

    def gather_sent():
        for h in range(2):
            every = omega[h].at[pl.ds(0, 56 * piece)]
            rcopy(every, every, gs.at[h], gr.at[h, 0], to_p).wait_send()

    def view(ch, side, src, n=1):
        if ch == 2:
            return labels.at[side, pl.ds(src, n)]
        return held.at[ch, side, pl.ds(src, n)]

    def along(src, ch, n, target):
        ref = view(ch, 0, src)
        return rcopy(ref, ref, zs.at[ch // 2], zr.at[ch, n], target)

    def parts(src, ch, n, target):
        if ch == 2:
            return [along(src, ch, n, target)]
        cuts = [pl.ds(0, head + 128), pl.ds(head + 128, 128 * (count - 1))]
        refs = [held.at[ch, 0, src, cut] for cut in cuts]
        sems = [zr.at[ch, n + 2 * k if n else 0] for k in range(2)]
        return [rcopy(a, a, zs.at[0], sem, target) for a, sem in zip(refs, sems)]

    def across(ch, src, n=1):
        rcopy(view(ch, 0, src, n), view(ch, 1, src, n), zs.at[ch // 2], zr.at[ch, 2], to_p).start()

    def launch(ch):
        @pl.when((f == 0) | (f == 3))
        def _():
            for cp in parts(f, ch, 1, to_two):
                cp.start()

        @pl.when((f == 1) | (f == 2))
        def _():
            along(f, ch, 0, to_two).start()

        @pl.when(f < 3)
        def _():
            along(f, ch, 0, right).start()

        @pl.when(f > 0)
        def _():
            along(f, ch, 0, left).start()

        across(ch, f)

    def relay(ch):
        @pl.when(f == 1)
        def _():
            for cp, on in zip(parts(3, ch, 1, left), parts(3, ch, 0, left)):
                cp.wait_recv()
                on.start()
            across(ch, 3)

        @pl.when(f == 2)
        def _():
            for cp, on in zip(parts(0, ch, 1, right), parts(0, ch, 0, right)):
                cp.wait_recv()
                on.start()
            across(ch, 0)

    def came(ch, amount):
        ref = view(ch, 0, 0, amount)
        rcopy(ref, ref, zs.at[ch // 2], zr.at[ch, 0], to_p).wait_recv()

    def collect(ch):
        @pl.when((f == 0) | (f == 3))
        def _():
            came(ch, 3)
            across(ch, 1 - f // 3, 3)

        @pl.when((f == 1) | (f == 2))
        def _():
            came(ch, 2)
            across(ch, f - 1)
            across(ch, f + 1)

    def paired(ch):
        ref = view(ch, 1, 0, 4)
        rcopy(ref, ref, zs.at[ch // 2], zr.at[ch, 2], to_p).wait_recv()

    def drained():
        def wait(buffer, n, sem):
            ref = buffer.at[..., pl.ds(0, n), :, :]
            rcopy(ref, ref, zs.at[sem], zr.at[0, 0], to_p).wait_send()

        @pl.when((f == 0) | (f == 3))
        def _():
            wait(held, 3, 0)
            wait(labels, 3, 1)

        @pl.when((f == 1) | (f == 2))
        def _():
            wait(held, 4, 0)
            wait(labels, 4, 1)

    gather_own(0)
    for cp in small:
        cp.wait()
    at_row = lax.broadcasted_iota(jnp.int32, (8, 128), 0)
    own_labels = jnp.zeros((8, 128), jnp.int32)
    for t in range(count):
        label = front_ref[t] * row_tiles + tile_ref[t]
        own_labels = jnp.where(at_row == t, label, own_labels)
    labels[0, f] = own_labels
    launch(2)
    for i in range(4):
        gather_near(0, i)
    gather_own(1)
    gather_rest(0)
    relay(2)
    gather_far(0, 0)
    gather_z(0)
    collect(2)
    gather_far(0, 1)
    gather_pair(0)
    loads[0].wait()

    def product(h, t):
        acc = jnp.zeros((128, half), F32)
        for b in range(0, column_ref.shape[1], 2):
            chosen = jnp.concatenate([omega[h][column_ref[t, b + g]] for g in range(2)], axis=0)
            acc = acc + jnp.dot(
                child[t, :, 128 * b : 128 * (b + 2)], chosen, preferred_element_type=F32
            )
        return acc

    def pack(ref, tiles):
        codes = [code_of(tile) for tile in tiles]
        ref[:head, :] = jnp.concatenate(codes, axis=0).astype(jnp.int32).astype(jnp.int16)
        for t, tile in enumerate(tiles):
            at = head + 128 * t
            ref[at : at + 128, :] = coded(tile, codes[t])

    def unpack(ref, t):
        at = head + 128 * t
        return decoded(ref[at : at + 128, :], step_of(ref[:head, :])[8 * t : 8 * t + 8])

    def direct(h):
        @pl.loop(0, slab_rows // 128)
        def _(i):
            rows = pl.ds(pl.multiple_of(i * 128, 128), 128)
            part[h, rows, :] = jnp.dot(
                slab[rows, :],
                omega[h][pl.ds(c * (slab_cols // 128), slab_cols // 128)].reshape(slab_cols, half),
                preferred_element_type=F32,
            )

    gather_near(1, 0)
    pack(held.at[0, 0, f], [product(0, t) for t in range(count)])
    launch(0)
    for i in range(1, 4):
        gather_near(1, i)
    paired(2)
    to_smem = pltpu.make_async_copy(labels, label_ref, copy_sem.at[7])
    to_smem.start()
    loads[1].wait()
    direct(0)
    to_smem.wait()

    sources = [(side, s, t) for s in range(4) for side in range(2) for t in range(count)]
    none = len(sources)
    known = [label_ref[side, s, t, 0] for side, s, t in sources]
    before = []
    for n, label in enumerate(known):
        prev = jnp.int32(none)
        for m in range(n):
            prev = jnp.where(known[m] == label, m, prev)
        before.append(prev)

    def last_of(row, col, j):
        wanted = f * row_tiles + (row * 2 + col) * pieces + j
        last = jnp.int32(none)
        for n, label in enumerate(known):
            last = jnp.where(label == wanted, n, last)
        return last

    spots = [(r_x, 1 - c), (r_x, c), (r, 1 - c), (r, c)]
    lasts = [[last_of(row, col, j) for j in range(pieces)] for row, col in spots]

    gather_rest(1)
    gather_z(1)
    relay(0)
    gather_far(1, 0)
    gather_far(1, 1)
    gather_pair(1)
    pack(held.at[1, 0, f], [product(1, t) for t in range(count)])
    launch(1)
    sums[none] = jnp.zeros((128, half), F32)

    def accumulate(h):
        for n, (side, s, t) in enumerate(sources):
            sums[n] = unpack(held.at[h, side, s], t) + sums[before[n]]

    def block(h, n, j):
        row, col = spots[n]
        total = sums[lasts[n][j]]
        if n >= 2:
            at = pl.multiple_of(col * own_rows + j * 128, 128)
            total = total + part[h, pl.ds(at, 128), :]
        return total

    def hop(h, n):
        target = (to_d, to_x, to_y)[n]
        return rcopy(blocks.at[h, n], got.at[h, n], es.at[0], er.at[h], target)

    def spread(h):
        for n in range(3):
            pack(blocks.at[h, n], [block(h, n, j) for j in range(pieces)])
            hop(h, n).start()
        for j in range(pieces):
            sampled_ref[128 * j : 128 * (j + 1), h * half : (h + 1) * half] = block(h, 3, j)

    def finish(h):
        rcopy(got.at[h], got.at[h], es.at[0], er.at[h], to_p).wait_recv()
        for j in range(pieces):
            total = sampled_ref[128 * j : 128 * (j + 1), h * half : (h + 1) * half]
            for n in range(3):
                total = total + unpack(got.at[h, n], j)
            sampled_ref[128 * j : 128 * (j + 1), h * half : (h + 1) * half] = total

    def masked(h):
        lane = lax.broadcasted_iota(jnp.int32, (own_rows, half), 1) + h * half
        return jnp.where(lane < rank_ref[0], sampled_ref[:, h * half : (h + 1) * half], 0.0)

    def gram_hop(n):
        return rcopy(gram_own.at[n], gram_got.at[n], es.at[1], er.at[2 + n], to_y)

    def gram_send(n, i, j):
        gram_own[n] = lax.dot_general(
            masked(i),
            masked(j),
            (((0,), (0,)), ((), ())),
            precision=HI,
            preferred_element_type=F32,
        )
        gram_hop(n).start()

    def gram_total(n):
        gram_hop(n).wait_recv()
        total = gram_own[n] + gram_got[n]
        if n == 1:
            return total
        row = lax.broadcasted_iota(jnp.int32, (half, half), 0)
        lane = lax.broadcasted_iota(jnp.int32, (half, half), 1)
        beyond = (row == lane) & (lane + (n // 2) * half >= rank_ref[0])
        return total + jnp.where(beyond, 1.0, 0.0)

    collect(0)
    paired(0)
    accumulate(0)
    spread(0)
    direct(1)
    relay(1)
    collect(1)
    paired(1)
    accumulate(1)
    spread(1)
    finish(0)
    gram_send(0, 0, 0)
    finish(1)
    gram_send(1, 1, 0)
    gram_send(2, 1, 1)
    gram = gram_total(0)
    inv1 = inverse_factor(gram)
    low = dot_nt(gram_total(1), inv1)
    inv2 = inverse_factor(gram_total(2) - dot_nt(low, low))
    basis = dot_nt(masked(0), inv1)
    basis_ref[:, :half] = basis
    basis_ref[:, half:] = dot_nt(masked(1) - dot_nt(basis, low), inv2)
    gather_sent()
    drained()
    rcopy(blocks, got, es.at[0], er.at[0], to_p).wait_send()
    rcopy(gram_own, gram_got, es.at[1], er.at[0], to_p).wait_send()


def sampled_and_bases(
    slab, samples, child_tiles, parent_front, parent_tile, column_tiles, ranks
):
    width = samples.shape[1]
    half = width // 2
    count = child_tiles.shape[0]
    rows = slab.shape[0] // 2
    hbm = pl.BlockSpec(memory_space=pl.ANY)
    vmem = pl.BlockSpec(memory_space=pltpu.VMEM)
    dma = lambda *n: pltpu.SemaphoreType.DMA(n)
    parent_front, ranks = parent_front.reshape(-1), ranks.reshape(-1)
    return pl.pallas_call(
        sample_kernel,
        out_shape=(jax.ShapeDtypeStruct((rows, width), F32),) * 2,
        in_specs=[hbm] * 7,
        out_specs=(vmem, vmem),
        scratch_shapes=[
            pltpu.SMEM(parent_tile.shape, jnp.int32),
            pltpu.SMEM(parent_front.shape, jnp.int32),
            pltpu.SMEM(column_tiles.shape, jnp.int32),
            pltpu.SMEM(ranks.shape, jnp.int32),
            pltpu.VMEM((samples.shape[0] // 128 * 8, 128, half), samples.dtype),
            pltpu.VMEM((samples.shape[0] // 128 * 8, 128, half), samples.dtype),
            pltpu.VMEM(slab.shape, slab.dtype),
            pltpu.VMEM(child_tiles.shape, child_tiles.dtype),
            pltpu.VMEM((2, 4, 8, 128), jnp.int32),
            pltpu.SMEM((2, 4, 8, 128), jnp.int32),
            pltpu.VMEM((2, 2, 4, 136 * count, half), jnp.int16),
            pltpu.VMEM((8 * count + 1, 128, half), F32),
            pltpu.VMEM((2, slab.shape[0], half), F32),
            pltpu.VMEM((2, 3, 8 * count + rows, half), jnp.int16),
            pltpu.VMEM((2, 3, 8 * count + rows, half), jnp.int16),
            pltpu.VMEM((3, half, half), F32),
            pltpu.VMEM((3, half, half), F32),
            dma(10),
            dma(2),
            dma(2, 13),
            dma(2),
            dma(3, 4),
            dma(2),
            dma(5),
        ],
        compiler_params=pltpu.CompilerParams(
            collective_id=0, has_side_effects=True, vmem_limit_bytes=48 * 1024 * 1024
        ),
        name="sampled_and_bases",
    )(
        *[
            a if a is ranks else pltpu.with_memory_space_constraint(a, pltpu.HBM)
            for a in (
                parent_tile,
                parent_front,
                column_tiles,
                ranks,
                slab,
                samples.reshape(-1, 128, width),
                child_tiles,
            )
        ]
    )


def sampled_and_gram_any(
    slab, samples, child_tiles, parent_front, parent_tile, column_tiles, ranks
):
    width = samples.shape[1]
    half = width // 2
    col_width = slab.shape[1]
    omega = lax.all_gather(samples, ("row", "col"), axis=0, tiled=True)
    own = lax.dynamic_slice_in_dim(omega, lax.axis_index("col") * col_width, col_width, 0)
    direct = lax.psum_scatter(
        jnp.dot(slab, own, preferred_element_type=F32), "col", scatter_dimension=0, tiled=True
    )
    count = child_tiles.shape[0]
    blocks = child_tiles.shape[2] // 128
    chosen = omega.reshape(-1, 128, width)[column_tiles]
    pieces = child_tiles.reshape(count, 128, blocks, 128)
    product = jnp.einsum("trkc,tkcs->trs", pieces, chosen, preferred_element_type=F32)
    row_tiles = slab.shape[0] * lax.axis_size("row") // 128
    label = (parent_front[:, 0] * row_tiles + parent_tile).astype(F32)
    product = lax.all_gather(product, "front", axis=0, tiled=True)
    label = lax.all_gather(label, "front", axis=0, tiled=True)
    wanted = (lax.axis_index("front") * row_tiles + jnp.arange(row_tiles)).astype(F32)
    spread = (label[:, None] == wanted[None, :]).astype(F32)
    rows_full = jnp.einsum("qj,qrs->jrs", spread, product, precision=HI)
    rows_full = rows_full.reshape(row_tiles * 128, width)
    extended = lax.psum_scatter(rows_full, ("row", "col"), scatter_dimension=0, tiled=True)
    sampled = direct + extended
    masked = jnp.where(jnp.arange(width)[None, :] < ranks[0, 0], sampled, 0.0)
    gram = lax.psum(jnp.dot(masked.T, masked, precision=HI), "col")
    gram = jnp.stack([gram[:half, :half], gram[half:, :half], gram[half:, half:]])
    rank = jnp.broadcast_to(ranks.astype(F32)[:, :, None], (3, 8, half))
    return sampled, jnp.concatenate([gram, rank], axis=1)


def on_device(
    sizes, front_slab, samples, child_tiles, parent_front, parent_tile, column_tiles, ranks
):
    args = (samples, child_tiles, parent_front, parent_tile, column_tiles, ranks)
    tiles, count = samples.shape[0] // 128, child_tiles.shape[0]
    near = sizes["row"] == 4 and sizes["col"] == 2 and sizes["front"] == 4
    if near and tiles % 8 == 0 and count == 2 and front_slab.shape[1] == 512:
        sampled, basis = sampled_and_bases(front_slab[0], *args)
    else:
        sampled, gram = sampled_and_gram_any(front_slab[0], *args)
        sampled, basis = leaf_bases(sampled, gram)
    return (sampled[None], basis[None])


def solution(mesh):
    in_specs = (
        P("front", "row", "col"),
        P(("row", "col"), None),
        P(("front", "row", "col"), None, None),
        P(("front", "row", "col"), None),
        P(("front", "row", "col")),
        P(("front", "row", "col"), None),
        P("front", "row"),
    )
    out_specs = (P("front", ("row", "col"), None), P("front", ("row", "col"), None))
    return jax.shard_map(
        functools.partial(on_device, dict(mesh.shape)),
        mesh=mesh,
        in_specs=in_specs,
        out_specs=out_specs,
        check_vma=False,
    )
```

```python
import functools

import jax
import jax.numpy as jnp
from jax import lax
from jax.experimental import pallas as pl
from jax.experimental.pallas import tpu as pltpu
from jax.sharding import PartitionSpec as P

F32 = jnp.float32
HI = lax.Precision.HIGHEST
LOGICAL = pl.DeviceIdType.MESH


def dot_nt(a, b):
    return lax.dot_general(a, b, (((1,), (1,)), ((), ())), precision=HI, preferred_element_type=F32)


def row_of(x, k):
    return jnp.broadcast_to(x[k : k + 1, :], (8, x.shape[1]))
def inverse_factor(a, B=2):
    n = a.shape[0]
    r = lax.broadcasted_iota(jnp.int32, (n, n), 0)
    l = lax.broadcasted_iota(jnp.int32, (n, n), 1)
    diagonal = jnp.where(r == l, a, 0.0)
    across = lax.rsqrt(jnp.sum(diagonal, axis=0, keepdims=True))
    down = lax.rsqrt(jnp.sum(diagonal, axis=1, keepdims=True))
    a = a * across * down
    w = [a[8 * t : 8 * t + 8, :] for t in range(n // 8)]
    lane = lax.broadcasted_iota(jnp.int32, (8, n), 1)
    sub = lax.broadcasted_iota(jnp.int32, (8, n), 0)
    at = [sub == k for k in range(8)]
    size = 8 * B
    rows = []
    for first in range(0, n // 8, B):
        base = 8 * first
        inside = (lane >= base) & (lane < base + size)
        mine = w[first : first + B]
        cols = [[jnp.broadcast_to(x[:, base + k : base + k + 1], (8, n)) for x in mine] for k in range(size)]
        v = [jnp.where(inside, jnp.where(lane - base - 8 * t == sub, 1.0, 0.0), x) for t, x in enumerate(mine)]
        done = [None] * B
        pivots = [None] * B
        for k in range(0, size, 2):
            t, s = k // 8, k % 8
            left, right = cols[k], cols[k + 1]
            p, q, u = row_of(left[t], s), row_of(right[t], s), row_of(right[t], s + 1)
            det = p * u - q * q
            inv = 1.0 / det
            ratio = 1.0 / p
            v0, v1 = row_of(v[t], s), row_of(v[t], s + 1)
            second = v1 - (q * ratio) * v0
            if s == 0:
                done[t], pivots[t] = v0, p
            else:
                done[t] = jnp.where(at[s], v0, done[t])
                pivots[t] = jnp.where(at[s], p, pivots[t])
            done[t] = jnp.where(at[s + 1], second, done[t])
            pivots[t] = jnp.where(at[s + 1], det * ratio, pivots[t])

            def step(x, x0, x1):
                y0 = u * x0 - q * x1
                y1 = p * x1 - q * x0
                out = [x[i] - (left[i] * y0 + right[i] * y1) * inv for i in range(B)]
                out[t] = jnp.where(at[s], y0 * inv, jnp.where(at[s + 1], y1 * inv, out[t]))
                return out

            v = step(v, v0, v1)
            for m in range(k + 2, size):
                cols[m] = step(cols[m], row_of(cols[m][t], s), row_of(cols[m][t], s + 1))
        for t in range(B):
            rows.append(jnp.where(lane < base + 8 * (t + 1), done[t], 0.0) * lax.rsqrt(pivots[t]) * across)
        vk = [row_of(v[k // 8], k % 8) for k in range(size)]
        for i in range(first + B, n // 8):
            terms = [jnp.broadcast_to(w[i][:, base + k : base + k + 1], (8, n)) * vk[k] for k in range(size)]
            while len(terms) > 1:
                terms = [x + y for x, y in zip(terms[::2], terms[1::2])]
            w[i] = jnp.where(inside, 0.0, w[i]) - terms[0]
    return jnp.concatenate(rows, axis=0)


def basis_kernel(sampled_ref, gram_ref, out_ref, basis_ref):
    half = gram_ref.shape[2]
    rank = gram_ref[0, half : half + 1, :]
    sampled = sampled_ref[...]
    out_ref[...] = sampled
    rows = sampled.shape[0]
    lane = lax.broadcasted_iota(jnp.int32, (rows, half), 1).astype(F32)
    first = jnp.where(lane < rank, sampled[:, :half], 0.0)
    second = jnp.where(lane + half < rank, sampled[:, half:], 0.0)
    r = lax.broadcasted_iota(jnp.int32, (half, half), 0)
    c = lax.broadcasted_iota(jnp.int32, (half, half), 1)
    lane = c.astype(F32)
    a = gram_ref[0, :half, :] + jnp.where((r == c) & (lane >= rank), 1.0, 0.0)
    inv1 = inverse_factor(a)
    low = dot_nt(gram_ref[1, :half, :], inv1)
    a = gram_ref[2, :half, :] + jnp.where((r == c) & (lane + half >= rank), 1.0, 0.0)
    a = a - dot_nt(low, low)
    inv2 = inverse_factor(a)
    basis = dot_nt(first, inv1)
    basis_ref[:, :half] = basis
    basis_ref[:, half:] = dot_nt(second - dot_nt(basis, low), inv2)


def leaf_bases(sampled, gram):
    vmem = pl.BlockSpec(memory_space=pltpu.VMEM)
    return pl.pallas_call(
        basis_kernel,
        out_shape=(jax.ShapeDtypeStruct(sampled.shape, F32),) * 2,
        in_specs=[vmem, vmem],
        out_specs=(vmem, vmem),
        name="leaf_bases",
    )(sampled, gram)


LEVELS = 32767.0


def widened(code):
    return code.astype(jnp.int32).astype(F32)


def step_of(code):
    return jnp.exp2(widened(code) * (1.0 / 256.0)) * (1.0 / LEVELS)


def code_of(block):
    peak = jnp.max(jnp.max(jnp.abs(block), axis=0, keepdims=True), axis=1, keepdims=True)
    peak = jnp.broadcast_to(jnp.maximum(peak, 1e-30), (8, 128))
    return jnp.ceil(jnp.log2(peak) * 256.0) + 2.0


def coded(block, code):
    rows, lanes = block.shape
    scale = jnp.exp2(code * (-1.0 / 256.0)) * LEVELS
    scaled = (block.reshape(rows // 8, 8, lanes) * scale[None]).reshape(rows, lanes)
    return jnp.round(scaled).astype(jnp.int32).astype(jnp.int16)


def decoded(words, step):
    rows, lanes = words.shape
    values = widened(words).reshape(rows // 8, 8, lanes) * step[None]
    return values.reshape(rows, lanes)


def sample_kernel(
    tile_hbm,
    front_hbm,
    column_hbm,
    rank_ref,
    slab_ref,
    samples_ref,
    child_ref,
    out_ref,
    tile_ref,
    front_ref,
    column_ref,
    omega_low,
    omega_high,
    slab,
    child,
    labels,
    label_ref,
    held,
    sums,
    part,
    blocks,
    got,
    gram_own,
    gram_got,
    copy_sem,
    gs,
    gr,
    zs,
    zr,
    es,
    er,
):
    f, r, c = lax.axis_index("front"), lax.axis_index("row"), lax.axis_index("col")
    omega = (omega_low, omega_high)
    sampled_ref, basis_ref = out_ref.at[0], out_ref.at[1]
    x, core = r // 2, r % 2
    width = samples_ref.shape[2]
    half = width // 2
    chunk = samples_ref.shape[0]
    piece = chunk // 8
    odd = f % 2
    count = child_ref.shape[0]
    slab_rows, slab_cols = slab_ref.shape
    own_rows = slab_rows // 2
    pieces = own_rows // 128
    row_tiles = slab_rows * 4 // 128
    head = 8 * count
    r_x = (1 - x) * 2 + core
    r_p = x * 2 + (1 - core)
    r_d = (1 - x) * 2 + (1 - core)
    to_x, to_y, to_p, to_d = (f, r_x, c), (f, r, 1 - c), (f, r_p, c), (f, r_x, 1 - c)
    right, left = (f + 1, r, c), (f - 1, r, c)
    to_z, to_two = (f + 1 - 2 * odd, r, c), ((f + 2) % 4, r, c)
    base = (r * 2 + c) * chunk

    loads = [
        pltpu.make_async_copy(child_ref, child, copy_sem.at[0]),
        pltpu.make_async_copy(slab_ref, slab, copy_sem.at[1]),
    ]
    own_loads = [
        pltpu.make_async_copy(
            samples_ref.at[:, :, pl.ds(h * half, half)],
            omega[h].at[pl.ds(base, chunk)],
            copy_sem.at[8 + h],
        )
        for h in range(2)
    ]
    small = [
        pltpu.make_async_copy(src, dst, copy_sem.at[3 + n])
        for n, (src, dst) in enumerate(
            (
                (tile_hbm, tile_ref),
                (front_hbm, front_ref),
                (column_hbm, column_ref),
            )
        )
    ]
    for cp in own_loads + small:
        cp.start()
    loads[0].start()
    loads[1].start()

    barrier = pltpu.get_barrier_semaphore()
    for target in (to_x, to_y, to_p, to_d, to_two):
        pl.semaphore_signal(barrier, inc=1, device_id=target, device_id_type=LOGICAL)

    @pl.when(f < 3)
    def _():
        pl.semaphore_signal(barrier, inc=1, device_id=right, device_id_type=LOGICAL)

    @pl.when(f > 0)
    def _():
        pl.semaphore_signal(barrier, inc=1, device_id=left, device_id_type=LOGICAL)

    pl.semaphore_wait(barrier, 5 + jnp.minimum(f, 1) + jnp.minimum(3 - f, 1))

    def rcopy(src, dst, send, recv, target):
        return pltpu.make_async_remote_copy(
            src_ref=src,
            dst_ref=dst,
            send_sem=send,
            recv_sem=recv,
            device_id=target,
            device_id_type=LOGICAL,
        )

    def place(h, row, col, i, n=1):
        start = (row * 2 + col) * chunk + (i + odd * (8 - n - 2 * i)) * piece
        return omega[h].at[pl.ds(start, n * piece)]

    via_z = (3, 1)

    def send(h, ref, n, target):
        rcopy(ref, ref, gs.at[h], gr.at[h, n], target).start()

    def arrived(h, ref, n):
        rcopy(ref, ref, gs.at[h], gr.at[h, n], to_p).wait_recv()

    def all_arrived(h, amount, n):
        arrived(h, omega[h].at[pl.ds(0, amount * piece)], n)

    def pair_up(h, row, col, i, n=1):
        send(h, place(h, row, col, i, n), 12, to_p)

    def gather_own(h):
        own_loads[h].wait()
        for i in range(8 - via_z[h]):
            send(h, place(h, r, c, i), i if i < 4 else 8, to_x)
            send(h, place(h, r, c, 7 - i), 4 + i if i < 4 else 8, to_y)
        pair_up(h, r, c, 0, 8)

    def gather_near(h, i):
        ref = place(h, r_x, c, i)
        arrived(h, ref, i)
        if i < via_z[h]:
            send(h, ref, 9, to_z)
        send(h, ref, 10 + i // 2, to_y)
        pair_up(h, r_x, c, i)
        ref = place(h, r, 1 - c, 7 - i)
        arrived(h, ref, 4 + i)
        if i < via_z[h]:
            send(h, ref, 9, to_z)
        send(h, ref, 10 + i // 2, to_x)
        pair_up(h, r, 1 - c, 7 - i)

    def gather_rest(h):
        n = 4 - via_z[h]
        all_arrived(h, 2 * n, 8)
        pair_up(h, r_x, c, 4, n)
        pair_up(h, r, 1 - c, 4 - n, n)

    def gather_z(h):
        n = via_z[h]
        all_arrived(h, 2 * n, 9)
        pair_up(h, r_x, c, 8 - n, n)
        pair_up(h, r, 1 - c, 0, n)

    def gather_far(h, g):
        all_arrived(h, 4, 10 + g)
        pair_up(h, r_x, 1 - c, 2 * g, 2)
        pair_up(h, r_x, 1 - c, 6 - 2 * g, 2)

    def gather_pair(h):
        all_arrived(h, 32, 12)

    def gather_sent():
        for h in range(2):
            every = omega[h].at[pl.ds(0, 56 * piece)]
            rcopy(every, every, gs.at[h], gr.at[h, 0], to_p).wait_send()

    def view(ch, side, src, n=1):
        if ch == 2:
            return labels.at[side, pl.ds(src, n)]
        return held.at[ch, side, pl.ds(src, n)]

    def along(src, ch, n, target):
        ref = view(ch, 0, src)
        return rcopy(ref, ref, zs.at[ch // 2], zr.at[ch, n], target)

    def parts(src, ch, n, target):
        if ch == 2:
            return [along(src, ch, n, target)]
        cuts = [pl.ds(0, head + 128), pl.ds(head + 128, 128 * (count - 1))]
        refs = [held.at[ch, 0, src, cut] for cut in cuts]
        sems = [zr.at[ch, n + 2 * k if n else 0] for k in range(2)]
        return [rcopy(a, a, zs.at[0], sem, target) for a, sem in zip(refs, sems)]

    def across(ch, src, n=1):
        rcopy(view(ch, 0, src, n), view(ch, 1, src, n), zs.at[ch // 2], zr.at[ch, 2], to_p).start()

    def launch(ch):
        @pl.when((f == 0) | (f == 3))
        def _():
            for cp in parts(f, ch, 1, to_two):
                cp.start()

        @pl.when((f == 1) | (f == 2))
        def _():
            along(f, ch, 0, to_two).start()

        @pl.when(f < 3)
        def _():
            along(f, ch, 0, right).start()

        @pl.when(f > 0)
        def _():
            along(f, ch, 0, left).start()

        across(ch, f)

    def relay(ch):
        @pl.when(f == 1)
        def _():
            for cp, on in zip(parts(3, ch, 1, left), parts(3, ch, 0, left)):
                cp.wait_recv()
                on.start()
            across(ch, 3)

        @pl.when(f == 2)
        def _():
            for cp, on in zip(parts(0, ch, 1, right), parts(0, ch, 0, right)):
                cp.wait_recv()
                on.start()
            across(ch, 0)

    def came(ch, amount):
        ref = view(ch, 0, 0, amount)
        rcopy(ref, ref, zs.at[ch // 2], zr.at[ch, 0], to_p).wait_recv()

    def collect(ch):
        @pl.when((f == 0) | (f == 3))
        def _():
            came(ch, 3)
            across(ch, 1 - f // 3, 3)

        @pl.when((f == 1) | (f == 2))
        def _():
            came(ch, 2)
            across(ch, f - 1)
            across(ch, f + 1)

    def paired(ch):
        ref = view(ch, 1, 0, 4)
        rcopy(ref, ref, zs.at[ch // 2], zr.at[ch, 2], to_p).wait_recv()

    def drained():
        def wait(buffer, n, sem):
            ref = buffer.at[..., pl.ds(0, n), :, :]
            rcopy(ref, ref, zs.at[sem], zr.at[0, 0], to_p).wait_send()

        @pl.when((f == 0) | (f == 3))
        def _():
            wait(held, 3, 0)
            wait(labels, 3, 1)

        @pl.when((f == 1) | (f == 2))
        def _():
            wait(held, 4, 0)
            wait(labels, 4, 1)

    gather_own(0)
    for cp in small:
        cp.wait()
    at_row = lax.broadcasted_iota(jnp.int32, (8, 128), 0)
    own_labels = jnp.zeros((8, 128), jnp.int32)
    for t in range(count):
        label = front_ref[t] * row_tiles + tile_ref[t]
        own_labels = jnp.where(at_row == t, label, own_labels)
    labels[0, f] = own_labels
    launch(2)
    for i in range(4):
        gather_near(0, i)
    gather_own(1)
    gather_rest(0)
    relay(2)
    gather_far(0, 0)
    gather_z(0)
    collect(2)
    gather_far(0, 1)
    gather_pair(0)
    loads[0].wait()

    def product(h, t):
        acc = jnp.zeros((128, half), F32)
        for b in range(0, column_ref.shape[1], 2):
            chosen = jnp.concatenate([omega[h][column_ref[t, b + g]] for g in range(2)], axis=0)
            acc = acc + jnp.dot(
                child[t, :, 128 * b : 128 * (b + 2)], chosen, preferred_element_type=F32
            )
        return acc

    def pack(ref, tiles):
        codes = [code_of(tile) for tile in tiles]
        ref[:head, :] = jnp.concatenate(codes, axis=0).astype(jnp.int32).astype(jnp.int16)
        for t, tile in enumerate(tiles):
            at = head + 128 * t
            ref[at : at + 128, :] = coded(tile, codes[t])

    def unpack(ref, t):
        at = head + 128 * t
        return decoded(ref[at : at + 128, :], step_of(ref[:head, :])[8 * t : 8 * t + 8])

    def direct(h, low, high):
        @pl.loop(low, high)
        def _(i):
            rows = pl.ds(pl.multiple_of(i * 128, 128), 128)
            part[h, rows, :] = jnp.dot(
                slab[rows, :],
                omega[h][pl.ds(c * (slab_cols // 128), slab_cols // 128)].reshape(slab_cols, half),
                preferred_element_type=F32,
            )

    gather_near(1, 0)
    pack(held.at[0, 0, f], [product(0, t) for t in range(count)])
    launch(0)
    for i in range(1, 4):
        gather_near(1, i)
    paired(2)
    to_smem = pltpu.make_async_copy(labels, label_ref, copy_sem.at[7])
    to_smem.start()
    loads[1].wait()
    direct(0, 0, slab_rows // 128)
    to_smem.wait()

    sources = [(side, s, t) for s in range(4) for side in range(2) for t in range(count)]
    none = len(sources)
    known = [label_ref[side, s, t, 0] for side, s, t in sources]
    before = []
    for n, label in enumerate(known):
        prev = jnp.int32(none)
        for m in range(n):
            prev = jnp.where(known[m] == label, m, prev)
        before.append(prev)

    def last_of(row, col, j):
        wanted = f * row_tiles + (row * 2 + col) * pieces + j
        last = jnp.int32(none)
        for n, label in enumerate(known):
            last = jnp.where(label == wanted, n, last)
        return last

    spots = [(r_x, 1 - c), (r_x, c), (r, 1 - c), (r, c)]
    lasts = [[last_of(row, col, j) for j in range(pieces)] for row, col in spots]

    gather_rest(1)
    gather_z(1)
    relay(0)
    gather_far(1, 0)
    gather_far(1, 1)
    gather_pair(1)
    pack(held.at[1, 0, f], [product(1, t) for t in range(count)])
    launch(1)
    sums[none] = jnp.zeros((128, half), F32)

    def accumulate(h):
        for n, (side, s, t) in enumerate(sources):
            sums[n] = unpack(held.at[h, side, s], t) + sums[before[n]]

    def block(h, n, j):
        row, col = spots[n]
        total = sums[lasts[n][j]]
        if n >= 2:
            at = pl.multiple_of(col * own_rows + j * 128, 128)
            total = total + part[h, pl.ds(at, 128), :]
        return total

    def hop(h, n):
        target = (to_d, to_x, to_y)[n]
        return rcopy(blocks.at[h, n], got.at[h, n], es.at[0], er.at[h], target)

    def spread(h):
        for n in range(3):
            pack(blocks.at[h, n], [block(h, n, j) for j in range(pieces)])
            hop(h, n).start()
        for j in range(pieces):
            sampled_ref[128 * j : 128 * (j + 1), h * half : (h + 1) * half] = block(h, 3, j)

    def finish(h):
        rcopy(got.at[h], got.at[h], es.at[0], er.at[h], to_p).wait_recv()
        for j in range(pieces):
            total = sampled_ref[128 * j : 128 * (j + 1), h * half : (h + 1) * half]
            for n in range(3):
                total = total + unpack(got.at[h, n], j)
            sampled_ref[128 * j : 128 * (j + 1), h * half : (h + 1) * half] = total

    def masked(h):
        lane = lax.broadcasted_iota(jnp.int32, (own_rows, half), 1) + h * half
        return jnp.where(lane < rank_ref[0], sampled_ref[:, h * half : (h + 1) * half], 0.0)

    def gram_hop(n):
        return rcopy(gram_own.at[n], gram_got.at[n], es.at[1], er.at[2 + n], to_y)

    def gram_send(n, i, j):
        gram_own[n] = lax.dot_general(
            masked(i),
            masked(j),
            (((0,), (0,)), ((), ())),
            precision=HI,
            preferred_element_type=F32,
        )
        gram_hop(n).start()

    def gram_total(n):
        gram_hop(n).wait_recv()
        total = gram_own[n] + gram_got[n]
        if n == 1:
            return total
        row = lax.broadcasted_iota(jnp.int32, (half, half), 0)
        lane = lax.broadcasted_iota(jnp.int32, (half, half), 1)
        beyond = (row == lane) & (lane + (n // 2) * half >= rank_ref[0])
        return total + jnp.where(beyond, 1.0, 0.0)

    collect(0)
    paired(0)
    accumulate(0)
    spread(0)
    direct(1, 0, slab_rows // 256)
    relay(1)
    direct(1, slab_rows // 256, slab_rows // 128)
    collect(1)
    paired(1)
    accumulate(1)
    spread(1)
    finish(0)
    gram_send(0, 0, 0)
    finish(1)
    gram_send(1, 1, 0)
    gram_send(2, 1, 1)
    inv1 = inverse_factor(gram_total(0))
    low = dot_nt(gram_total(1), inv1)
    gram = gram_total(2) - dot_nt(low, low)
    basis = dot_nt(masked(0), inv1)
    basis_ref[:, :half] = basis
    rest = masked(1) - dot_nt(basis, low)
    basis_ref[:, half:] = dot_nt(rest, inverse_factor(gram))
    gather_sent()
    drained()
    rcopy(blocks, got, es.at[0], er.at[0], to_p).wait_send()
    rcopy(gram_own, gram_got, es.at[1], er.at[0], to_p).wait_send()


def sampled_and_bases(
    slab, samples, child_tiles, parent_front, parent_tile, column_tiles, ranks
):
    width = samples.shape[1]
    half = width // 2
    count = child_tiles.shape[0]
    rows = slab.shape[0] // 2
    hbm = pl.BlockSpec(memory_space=pl.ANY)
    vmem = pl.BlockSpec(memory_space=pltpu.VMEM)
    dma = lambda *n: pltpu.SemaphoreType.DMA(n)
    parent_front, ranks = parent_front.reshape(-1), ranks.reshape(-1)
    return pl.pallas_call(
        sample_kernel,
        out_shape=jax.ShapeDtypeStruct((2, rows, width), F32),
        in_specs=[hbm] * 3 + [pl.BlockSpec(memory_space=pltpu.SMEM)] + [hbm] * 3,
        out_specs=vmem,
        scratch_shapes=[
            pltpu.SMEM(parent_tile.shape, jnp.int32),
            pltpu.SMEM(parent_front.shape, jnp.int32),
            pltpu.SMEM(column_tiles.shape, jnp.int32),
            pltpu.VMEM((samples.shape[0] // 128 * 8, 128, half), samples.dtype),
            pltpu.VMEM((samples.shape[0] // 128 * 8, 128, half), samples.dtype),
            pltpu.VMEM(slab.shape, slab.dtype),
            pltpu.VMEM(child_tiles.shape, child_tiles.dtype),
            pltpu.VMEM((2, 4, 8, 128), jnp.int32),
            pltpu.SMEM((2, 4, 8, 128), jnp.int32),
            pltpu.VMEM((2, 2, 4, 136 * count, half), jnp.int16),
            pltpu.VMEM((8 * count + 1, 128, half), F32),
            pltpu.VMEM((2, slab.shape[0], half), F32),
            pltpu.VMEM((2, 3, 8 * count + rows, half), jnp.int16),
            pltpu.VMEM((2, 3, 8 * count + rows, half), jnp.int16),
            pltpu.VMEM((3, half, half), F32),
            pltpu.VMEM((3, half, half), F32),
            dma(10),
            dma(2),
            dma(2, 13),
            dma(2),
            dma(3, 4),
            dma(2),
            dma(5),
        ],
        compiler_params=pltpu.CompilerParams(
            collective_id=0, has_side_effects=True, vmem_limit_bytes=48 * 1024 * 1024
        ),
        name="sampled_and_bases",
    )(
        *[
            a if a is ranks else pltpu.with_memory_space_constraint(a, pltpu.HBM)
            for a in (
                parent_tile,
                parent_front,
                column_tiles,
                ranks,
                slab,
                samples.reshape(-1, 128, width),
                child_tiles,
            )
        ]
    )


def sampled_and_gram_any(
    slab, samples, child_tiles, parent_front, parent_tile, column_tiles, ranks
):
    width = samples.shape[1]
    half = width // 2
    col_width = slab.shape[1]
    omega = lax.all_gather(samples, ("row", "col"), axis=0, tiled=True)
    own = lax.dynamic_slice_in_dim(omega, lax.axis_index("col") * col_width, col_width, 0)
    direct = lax.psum_scatter(
        jnp.dot(slab, own, preferred_element_type=F32), "col", scatter_dimension=0, tiled=True
    )
    count = child_tiles.shape[0]
    blocks = child_tiles.shape[2] // 128
    chosen = omega.reshape(-1, 128, width)[column_tiles]
    pieces = child_tiles.reshape(count, 128, blocks, 128)
    product = jnp.einsum("trkc,tkcs->trs", pieces, chosen, preferred_element_type=F32)
    row_tiles = slab.shape[0] * lax.axis_size("row") // 128
    label = (parent_front[:, 0] * row_tiles + parent_tile).astype(F32)
    product = lax.all_gather(product, "front", axis=0, tiled=True)
    label = lax.all_gather(label, "front", axis=0, tiled=True)
    wanted = (lax.axis_index("front") * row_tiles + jnp.arange(row_tiles)).astype(F32)
    spread = (label[:, None] == wanted[None, :]).astype(F32)
    rows_full = jnp.einsum("qj,qrs->jrs", spread, product, precision=HI)
    rows_full = rows_full.reshape(row_tiles * 128, width)
    extended = lax.psum_scatter(rows_full, ("row", "col"), scatter_dimension=0, tiled=True)
    sampled = direct + extended
    masked = jnp.where(jnp.arange(width)[None, :] < ranks[0, 0], sampled, 0.0)
    gram = lax.psum(jnp.dot(masked.T, masked, precision=HI), "col")
    gram = jnp.stack([gram[:half, :half], gram[half:, :half], gram[half:, half:]])
    rank = jnp.broadcast_to(ranks.astype(F32)[:, :, None], (3, 8, half))
    return sampled, jnp.concatenate([gram, rank], axis=1)


def on_device(
    sizes, front_slab, samples, child_tiles, parent_front, parent_tile, column_tiles, ranks
):
    args = (samples, child_tiles, parent_front, parent_tile, column_tiles, ranks)
    tiles, count = samples.shape[0] // 128, child_tiles.shape[0]
    near = sizes["row"] == 4 and sizes["col"] == 2 and sizes["front"] == 4
    if near and tiles % 8 == 0 and count == 2 and front_slab.shape[1] == 512:
        sampled, basis = sampled_and_bases(front_slab[0], *args)
    else:
        sampled, gram = sampled_and_gram_any(front_slab[0], *args)
        sampled, basis = leaf_bases(sampled, gram)
    return (sampled[None], basis[None])


def solution(mesh):
    in_specs = (
        P("front", "row", "col"),
        P(("row", "col"), None),
        P(("front", "row", "col"), None, None),
        P(("front", "row", "col"), None),
        P(("front", "row", "col")),
        P(("front", "row", "col"), None),
        P("front", "row"),
    )
    out_specs = (P("front", ("row", "col"), None), P("front", ("row", "col"), None))
    return jax.shard_map(
        functools.partial(on_device, dict(mesh.shape)),
        mesh=mesh,
        in_specs=in_specs,
        out_specs=out_specs,
        check_vma=False,
    )
```

```python
import functools

import jax
import jax.numpy as jnp
from jax import lax
from jax.experimental import pallas as pl
from jax.experimental.pallas import tpu as pltpu
from jax.sharding import PartitionSpec as P

F32 = jnp.float32
HI = lax.Precision.HIGHEST
LOGICAL = pl.DeviceIdType.MESH


def dot_nt(a, b):
    return lax.dot_general(a, b, (((1,), (1,)), ((), ())), precision=HI, preferred_element_type=F32)


def row_of(x, k):
    return jnp.broadcast_to(x[k : k + 1, :], (8, x.shape[1]))
def inverse_factor(a, B=2):
    n = a.shape[0]
    r = lax.broadcasted_iota(jnp.int32, (n, n), 0)
    l = lax.broadcasted_iota(jnp.int32, (n, n), 1)
    diagonal = jnp.where(r == l, a, 0.0)
    across = lax.rsqrt(jnp.sum(diagonal, axis=0, keepdims=True))
    down = lax.rsqrt(jnp.sum(diagonal, axis=1, keepdims=True))
    a = a * across * down
    w = [a[8 * t : 8 * t + 8, :] for t in range(n // 8)]
    lane = lax.broadcasted_iota(jnp.int32, (8, n), 1)
    sub = lax.broadcasted_iota(jnp.int32, (8, n), 0)
    at = [sub == k for k in range(8)]
    size = 8 * B
    rows = []
    for first in range(0, n // 8, B):
        base = 8 * first
        inside = (lane >= base) & (lane < base + size)
        mine = w[first : first + B]
        cols = [[jnp.broadcast_to(x[:, base + k : base + k + 1], (8, n)) for x in mine] for k in range(size)]
        v = [jnp.where(inside, jnp.where(lane - base - 8 * t == sub, 1.0, 0.0), x) for t, x in enumerate(mine)]
        done = [None] * B
        pivots = [None] * B
        for k in range(0, size, 2):
            t, s = k // 8, k % 8
            left, right = cols[k], cols[k + 1]
            p, q, u = row_of(left[t], s), row_of(right[t], s), row_of(right[t], s + 1)
            det = p * u - q * q
            inv = 1.0 / det
            ratio = 1.0 / p
            v0, v1 = row_of(v[t], s), row_of(v[t], s + 1)
            second = v1 - (q * ratio) * v0
            if s == 0:
                done[t], pivots[t] = v0, p
            else:
                done[t] = jnp.where(at[s], v0, done[t])
                pivots[t] = jnp.where(at[s], p, pivots[t])
            done[t] = jnp.where(at[s + 1], second, done[t])
            pivots[t] = jnp.where(at[s + 1], det * ratio, pivots[t])

            def step(x, x0, x1):
                y0 = u * x0 - q * x1
                y1 = p * x1 - q * x0
                out = [x[i] - (left[i] * y0 + right[i] * y1) * inv for i in range(B)]
                out[t] = jnp.where(at[s], y0 * inv, jnp.where(at[s + 1], y1 * inv, out[t]))
                return out

            v = step(v, v0, v1)
            for m in range(k + 2, size):
                cols[m] = step(cols[m], row_of(cols[m][t], s), row_of(cols[m][t], s + 1))
        for t in range(B):
            rows.append(jnp.where(lane < base + 8 * (t + 1), done[t], 0.0) * lax.rsqrt(pivots[t]) * across)
        vk = [row_of(v[k // 8], k % 8) for k in range(size)]
        for i in range(first + B, n // 8):
            terms = [jnp.broadcast_to(w[i][:, base + k : base + k + 1], (8, n)) * vk[k] for k in range(size)]
            while len(terms) > 1:
                terms = [x + y for x, y in zip(terms[::2], terms[1::2])]
            w[i] = jnp.where(inside, 0.0, w[i]) - terms[0]
    return jnp.concatenate(rows, axis=0)


def basis_kernel(sampled_ref, gram_ref, out_ref, basis_ref):
    half = gram_ref.shape[2]
    rank = gram_ref[0, half : half + 1, :]
    sampled = sampled_ref[...]
    out_ref[...] = sampled
    rows = sampled.shape[0]
    lane = lax.broadcasted_iota(jnp.int32, (rows, half), 1).astype(F32)
    first = jnp.where(lane < rank, sampled[:, :half], 0.0)
    second = jnp.where(lane + half < rank, sampled[:, half:], 0.0)
    r = lax.broadcasted_iota(jnp.int32, (half, half), 0)
    c = lax.broadcasted_iota(jnp.int32, (half, half), 1)
    lane = c.astype(F32)
    a = gram_ref[0, :half, :] + jnp.where((r == c) & (lane >= rank), 1.0, 0.0)
    inv1 = inverse_factor(a)
    low = dot_nt(gram_ref[1, :half, :], inv1)
    a = gram_ref[2, :half, :] + jnp.where((r == c) & (lane + half >= rank), 1.0, 0.0)
    a = a - dot_nt(low, low)
    inv2 = inverse_factor(a)
    basis = dot_nt(first, inv1)
    basis_ref[:, :half] = basis
    basis_ref[:, half:] = dot_nt(second - dot_nt(basis, low), inv2)


def leaf_bases(sampled, gram):
    vmem = pl.BlockSpec(memory_space=pltpu.VMEM)
    return pl.pallas_call(
        basis_kernel,
        out_shape=(jax.ShapeDtypeStruct(sampled.shape, F32),) * 2,
        in_specs=[vmem, vmem],
        out_specs=(vmem, vmem),
        name="leaf_bases",
    )(sampled, gram)


LEVELS = 32767.0


def widened(code):
    return code.astype(jnp.int32).astype(F32)


def step_of(code):
    return jnp.exp2(widened(code) * (1.0 / 256.0)) * (1.0 / LEVELS)


def code_of(block):
    peak = jnp.max(jnp.max(jnp.abs(block), axis=0, keepdims=True), axis=1, keepdims=True)
    peak = jnp.broadcast_to(jnp.maximum(peak, 1e-30), (8, 128))
    return jnp.ceil(jnp.log2(peak) * 256.0) + 2.0


def coded(block, code):
    rows, lanes = block.shape
    scale = jnp.exp2(code * (-1.0 / 256.0)) * LEVELS
    scaled = (block.reshape(rows // 8, 8, lanes) * scale[None]).reshape(rows, lanes)
    return jnp.round(scaled).astype(jnp.int32).astype(jnp.int16)


def decoded(words, step):
    rows, lanes = words.shape
    values = widened(words).reshape(rows // 8, 8, lanes) * step[None]
    return values.reshape(rows, lanes)


def sample_kernel(
    tile_hbm,
    front_hbm,
    column_hbm,
    rank_ref,
    slab_ref,
    samples_ref,
    child_ref,
    out_ref,
    tile_ref,
    front_ref,
    column_ref,
    omega_low,
    omega_high,
    slab,
    child,
    labels,
    label_ref,
    held,
    sums,
    part,
    blocks,
    got,
    gram_own,
    gram_got,
    copy_sem,
    gs,
    gr,
    zs,
    zr,
    es,
    er,
):
    f, r, c = lax.axis_index("front"), lax.axis_index("row"), lax.axis_index("col")
    omega = (omega_low, omega_high)
    sampled_ref, basis_ref = out_ref.at[0], out_ref.at[1]
    x, core = r // 2, r % 2
    width = samples_ref.shape[2]
    half = width // 2
    chunk = samples_ref.shape[0]
    piece = chunk // 8
    odd = f % 2
    count = child_ref.shape[0]
    slab_rows, slab_cols = slab_ref.shape
    own_rows = slab_rows // 2
    pieces = own_rows // 128
    row_tiles = slab_rows * 4 // 128
    head = 8 * count
    r_x = (1 - x) * 2 + core
    r_p = x * 2 + (1 - core)
    r_d = (1 - x) * 2 + (1 - core)
    to_x, to_y, to_p, to_d = (f, r_x, c), (f, r, 1 - c), (f, r_p, c), (f, r_x, 1 - c)
    right, left = (f + 1, r, c), (f - 1, r, c)
    to_z, to_two = (f + 1 - 2 * odd, r, c), ((f + 2) % 4, r, c)
    base = (r * 2 + c) * chunk

    loads = [
        pltpu.make_async_copy(child_ref, child, copy_sem.at[0]),
        pltpu.make_async_copy(slab_ref, slab, copy_sem.at[1]),
    ]
    own_loads = [
        pltpu.make_async_copy(
            samples_ref.at[:, :, pl.ds(h * half, half)],
            omega[h].at[pl.ds(base, chunk)],
            copy_sem.at[8 + h],
        )
        for h in range(2)
    ]
    small = [
        pltpu.make_async_copy(src, dst, copy_sem.at[3 + n])
        for n, (src, dst) in enumerate(
            (
                (tile_hbm, tile_ref),
                (front_hbm, front_ref),
                (column_hbm, column_ref),
            )
        )
    ]
    for cp in own_loads + small:
        cp.start()
    loads[0].start()
    loads[1].start()

    barrier = pltpu.get_barrier_semaphore()
    for target in (to_x, to_y, to_p, to_d, to_two):
        pl.semaphore_signal(barrier, inc=1, device_id=target, device_id_type=LOGICAL)

    @pl.when(f < 3)
    def _():
        pl.semaphore_signal(barrier, inc=1, device_id=right, device_id_type=LOGICAL)

    @pl.when(f > 0)
    def _():
        pl.semaphore_signal(barrier, inc=1, device_id=left, device_id_type=LOGICAL)

    pl.semaphore_wait(barrier, 5 + jnp.minimum(f, 1) + jnp.minimum(3 - f, 1))

    def rcopy(src, dst, send, recv, target):
        return pltpu.make_async_remote_copy(
            src_ref=src,
            dst_ref=dst,
            send_sem=send,
            recv_sem=recv,
            device_id=target,
            device_id_type=LOGICAL,
        )

    def place(h, row, col, i, n=1):
        start = (row * 2 + col) * chunk + (i + odd * (8 - n - 2 * i)) * piece
        return omega[h].at[pl.ds(start, n * piece)]

    via_z = (3, 1)

    def send(h, ref, n, target):
        rcopy(ref, ref, gs.at[h], gr.at[h, n], target).start()

    def arrived(h, ref, n):
        rcopy(ref, ref, gs.at[h], gr.at[h, n], to_p).wait_recv()

    def all_arrived(h, amount, n):
        arrived(h, omega[h].at[pl.ds(0, amount * piece)], n)

    def pair_up(h, row, col, i, n=1):
        send(h, place(h, row, col, i, n), 8, to_p)

    def gather_own(h):
        own_loads[h].wait()
        for i in range(8 - via_z[h]):
            send(h, place(h, r, c, i), min(i, 4), to_x)
            send(h, place(h, r, c, 7 - i), min(i, 4), to_y)
        pair_up(h, r, c, 0, 8)

    def gather_near(h, i):
        all_arrived(h, 2, i)
        from_x, from_y = place(h, r_x, c, i), place(h, r, 1 - c, 7 - i)
        if i < via_z[h]:
            send(h, from_x, 5, to_z)
            send(h, from_y, 5, to_z)
        send(h, from_x, 6 + i // 2, to_y)
        send(h, from_y, 6 + i // 2, to_x)
        pair_up(h, r_x, c, i)
        pair_up(h, r, 1 - c, 7 - i)

    def gather_rest(h):
        n = 4 - via_z[h]
        all_arrived(h, 2 * n, 4)
        pair_up(h, r_x, c, 4, n)
        pair_up(h, r, 1 - c, 4 - n, n)

    def gather_z(h):
        n = via_z[h]
        all_arrived(h, 2 * n, 5)
        pair_up(h, r_x, c, 8 - n, n)
        pair_up(h, r, 1 - c, 0, n)

    def gather_far(h, g):
        all_arrived(h, 4, 6 + g)
        pair_up(h, r_x, 1 - c, 2 * g, 2)
        pair_up(h, r_x, 1 - c, 6 - 2 * g, 2)

    def gather_pair(h):
        all_arrived(h, 32, 8)

    def gather_sent():
        for h in range(2):
            every = omega[h].at[pl.ds(0, 56 * piece)]
            rcopy(every, every, gs.at[h], gr.at[h, 0], to_p).wait_send()

    def view(ch, side, src, n=1):
        if ch == 2:
            return labels.at[side, pl.ds(src, n)]
        return held.at[ch, side, pl.ds(src, n)]

    def along(src, ch, n, target):
        ref = view(ch, 0, src)
        return rcopy(ref, ref, zs.at[ch // 2], zr.at[ch, n], target)

    def parts(src, ch, n, target):
        if ch == 2:
            return [along(src, ch, n, target)]
        cuts = [pl.ds(0, head + 128), pl.ds(head + 128, 128 * (count - 1))]
        refs = [held.at[ch, 0, src, cut] for cut in cuts]
        sems = [zr.at[ch, n + 2 * k if n else 0] for k in range(2)]
        return [rcopy(a, a, zs.at[0], sem, target) for a, sem in zip(refs, sems)]

    def across(ch, src, n=1):
        rcopy(view(ch, 0, src, n), view(ch, 1, src, n), zs.at[ch // 2], zr.at[ch, 2], to_p).start()

    def launch(ch):
        @pl.when((f == 0) | (f == 3))
        def _():
            for cp in parts(f, ch, 1, to_two):
                cp.start()

        @pl.when((f == 1) | (f == 2))
        def _():
            along(f, ch, 0, to_two).start()

        @pl.when(f < 3)
        def _():
            along(f, ch, 0, right).start()

        @pl.when(f > 0)
        def _():
            along(f, ch, 0, left).start()

        across(ch, f)

    def relay(ch):
        @pl.when(f == 1)
        def _():
            for cp, on in zip(parts(3, ch, 1, left), parts(3, ch, 0, left)):
                cp.wait_recv()
                on.start()
            across(ch, 3)

        @pl.when(f == 2)
        def _():
            for cp, on in zip(parts(0, ch, 1, right), parts(0, ch, 0, right)):
                cp.wait_recv()
                on.start()
            across(ch, 0)

    def came(ch, amount):
        ref = view(ch, 0, 0, amount)
        rcopy(ref, ref, zs.at[ch // 2], zr.at[ch, 0], to_p).wait_recv()

    def collect(ch):
        @pl.when((f == 0) | (f == 3))
        def _():
            came(ch, 3)
            across(ch, 1 - f // 3, 3)

        @pl.when((f == 1) | (f == 2))
        def _():
            came(ch, 2)
            across(ch, f - 1)
            across(ch, f + 1)

    def paired(ch):
        ref = view(ch, 1, 0, 4)
        rcopy(ref, ref, zs.at[ch // 2], zr.at[ch, 2], to_p).wait_recv()

    def drained():
        def wait(buffer, n, sem):
            ref = buffer.at[..., pl.ds(0, n), :, :]
            rcopy(ref, ref, zs.at[sem], zr.at[0, 0], to_p).wait_send()

        @pl.when((f == 0) | (f == 3))
        def _():
            wait(held, 3, 0)
            wait(labels, 3, 1)

        @pl.when((f == 1) | (f == 2))
        def _():
            wait(held, 4, 0)
            wait(labels, 4, 1)

    gather_own(0)
    for cp in small:
        cp.wait()
    at_row = lax.broadcasted_iota(jnp.int32, (8, 128), 0)
    own_labels = jnp.zeros((8, 128), jnp.int32)
    for t in range(count):
        label = front_ref[t] * row_tiles + tile_ref[t]
        own_labels = jnp.where(at_row == t, label, own_labels)
    labels[0, f] = own_labels
    launch(2)
    for i in range(4):
        gather_near(0, i)
    gather_own(1)
    gather_rest(0)
    relay(2)
    gather_far(0, 0)
    gather_z(0)
    collect(2)
    gather_far(0, 1)
    gather_pair(0)
    loads[0].wait()

    def product(h, t):
        acc = jnp.zeros((128, half), F32)
        for b in range(0, column_ref.shape[1], 2):
            chosen = jnp.concatenate([omega[h][column_ref[t, b + g]] for g in range(2)], axis=0)
            acc = acc + jnp.dot(
                child[t, :, 128 * b : 128 * (b + 2)], chosen, preferred_element_type=F32
            )
        return acc

    def pack(ref, tiles):
        codes = [code_of(tile) for tile in tiles]
        ref[:head, :] = jnp.concatenate(codes, axis=0).astype(jnp.int32).astype(jnp.int16)
        for t, tile in enumerate(tiles):
            at = head + 128 * t
            ref[at : at + 128, :] = coded(tile, codes[t])

    def unpack(ref, t):
        at = head + 128 * t
        return decoded(ref[at : at + 128, :], step_of(ref[:head, :])[8 * t : 8 * t + 8])

    def direct(h, low, high):
        @pl.loop(low, high)
        def _(i):
            rows = pl.ds(pl.multiple_of(i * 128, 128), 128)
            part[h, rows, :] = jnp.dot(
                slab[rows, :],
                omega[h][pl.ds(c * (slab_cols // 128), slab_cols // 128)].reshape(slab_cols, half),
                preferred_element_type=F32,
            )

    gather_near(1, 0)
    pack(held.at[0, 0, f], [product(0, t) for t in range(count)])
    launch(0)
    for i in range(1, 4):
        gather_near(1, i)
    paired(2)
    to_smem = pltpu.make_async_copy(labels, label_ref, copy_sem.at[7])
    to_smem.start()
    loads[1].wait()
    direct(0, 0, slab_rows // 128)
    to_smem.wait()

    sources = [(side, s, t) for s in range(4) for side in range(2) for t in range(count)]
    none = len(sources)
    known = [label_ref[side, s, t, 0] for side, s, t in sources]
    before = []
    for n, label in enumerate(known):
        prev = jnp.int32(none)
        for m in range(n):
            prev = jnp.where(known[m] == label, m, prev)
        before.append(prev)

    def last_of(row, col, j):
        wanted = f * row_tiles + (row * 2 + col) * pieces + j
        last = jnp.int32(none)
        for n, label in enumerate(known):
            last = jnp.where(label == wanted, n, last)
        return last

    spots = [(r_x, 1 - c), (r, 1 - c), (r_x, c), (r, c)]
    lasts = [[last_of(row, col, j) for j in range(pieces)] for row, col in spots]

    gather_rest(1)
    gather_z(1)
    relay(0)
    gather_far(1, 0)
    gather_far(1, 1)
    gather_pair(1)
    pack(held.at[1, 0, f], [product(1, t) for t in range(count)])
    launch(1)
    sums[none] = jnp.zeros((128, half), F32)

    def accumulate(h):
        for n, (side, s, t) in enumerate(sources):
            sums[n] = unpack(held.at[h, side, s], t) + sums[before[n]]

    def block(h, n, j):
        row, col = spots[n]
        total = sums[lasts[n][j]]
        if n in (1, 3):
            at = pl.multiple_of(col * own_rows + j * 128, 128)
            total = total + part[h, pl.ds(at, 128), :]
        return total

    def hop(h, n):
        target = (to_d, to_y, to_x)[n]
        return rcopy(blocks.at[h, n], got.at[h, n], es.at[0], er.at[h], target)

    def spread(h):
        for n in range(3):
            pack(blocks.at[h, n], [block(h, n, j) for j in range(pieces)])
            hop(h, n).start()
        for j in range(pieces):
            sampled_ref[128 * j : 128 * (j + 1), h * half : (h + 1) * half] = block(h, 3, j)

    def finish(h):
        rcopy(got.at[h], got.at[h], es.at[0], er.at[h], to_p).wait_recv()
        for j in range(pieces):
            total = sampled_ref[128 * j : 128 * (j + 1), h * half : (h + 1) * half]
            for n in range(3):
                total = total + unpack(got.at[h, n], j)
            sampled_ref[128 * j : 128 * (j + 1), h * half : (h + 1) * half] = total

    def masked(h):
        lane = lax.broadcasted_iota(jnp.int32, (own_rows, half), 1) + h * half
        return jnp.where(lane < rank_ref[0], sampled_ref[:, h * half : (h + 1) * half], 0.0)

    def gram_hop(n):
        return rcopy(gram_own.at[n], gram_got.at[n], es.at[1], er.at[2 + n], to_y)

    def gram_send(n, i, j):
        gram_own[n] = lax.dot_general(
            masked(i),
            masked(j),
            (((0,), (0,)), ((), ())),
            precision=HI,
            preferred_element_type=F32,
        )
        gram_hop(n).start()

    def gram_total(n):
        gram_hop(n).wait_recv()
        total = gram_own[n] + gram_got[n]
        if n == 1:
            return total
        row = lax.broadcasted_iota(jnp.int32, (half, half), 0)
        lane = lax.broadcasted_iota(jnp.int32, (half, half), 1)
        beyond = (row == lane) & (lane + (n // 2) * half >= rank_ref[0])
        return total + jnp.where(beyond, 1.0, 0.0)

    collect(0)
    paired(0)
    accumulate(0)
    spread(0)
    direct(1, 0, slab_rows // 256)
    relay(1)
    direct(1, slab_rows // 256, slab_rows // 128)
    collect(1)
    paired(1)
    accumulate(1)
    spread(1)
    finish(0)
    gram_send(0, 0, 0)
    finish(1)
    gram_send(1, 1, 0)
    gram_send(2, 1, 1)
    inv1 = inverse_factor(gram_total(0))
    low = dot_nt(gram_total(1), inv1)
    gram = gram_total(2) - dot_nt(low, low)
    basis = dot_nt(masked(0), inv1)
    basis_ref[:, :half] = basis
    rest = masked(1) - dot_nt(basis, low)
    basis_ref[:, half:] = dot_nt(rest, inverse_factor(gram))
    gather_sent()
    drained()
    rcopy(blocks, got, es.at[0], er.at[0], to_p).wait_send()
    rcopy(gram_own, gram_got, es.at[1], er.at[0], to_p).wait_send()


def sampled_and_bases(
    slab, samples, child_tiles, parent_front, parent_tile, column_tiles, ranks
):
    width = samples.shape[1]
    half = width // 2
    count = child_tiles.shape[0]
    rows = slab.shape[0] // 2
    hbm = pl.BlockSpec(memory_space=pl.ANY)
    vmem = pl.BlockSpec(memory_space=pltpu.VMEM)
    dma = lambda *n: pltpu.SemaphoreType.DMA(n)
    parent_front, ranks = parent_front.reshape(-1), ranks.reshape(-1)
    return pl.pallas_call(
        sample_kernel,
        out_shape=jax.ShapeDtypeStruct((2, rows, width), F32),
        in_specs=[hbm] * 3 + [pl.BlockSpec(memory_space=pltpu.SMEM)] + [hbm] * 3,
        out_specs=vmem,
        scratch_shapes=[
            pltpu.SMEM(parent_tile.shape, jnp.int32),
            pltpu.SMEM(parent_front.shape, jnp.int32),
            pltpu.SMEM(column_tiles.shape, jnp.int32),
            pltpu.VMEM((samples.shape[0] // 128 * 8, 128, half), samples.dtype),
            pltpu.VMEM((samples.shape[0] // 128 * 8, 128, half), samples.dtype),
            pltpu.VMEM(slab.shape, slab.dtype),
            pltpu.VMEM(child_tiles.shape, child_tiles.dtype),
            pltpu.VMEM((2, 4, 8, 128), jnp.int32),
            pltpu.SMEM((2, 4, 8, 128), jnp.int32),
            pltpu.VMEM((2, 2, 4, 136 * count, half), jnp.int16),
            pltpu.VMEM((8 * count + 1, 128, half), F32),
            pltpu.VMEM((2, slab.shape[0], half), F32),
            pltpu.VMEM((2, 3, 8 * count + rows, half), jnp.int16),
            pltpu.VMEM((2, 3, 8 * count + rows, half), jnp.int16),
            pltpu.VMEM((3, half, half), F32),
            pltpu.VMEM((3, half, half), F32),
            dma(10),
            dma(2),
            dma(2, 9),
            dma(2),
            dma(3, 4),
            dma(2),
            dma(5),
        ],
        compiler_params=pltpu.CompilerParams(
            collective_id=0, has_side_effects=True, vmem_limit_bytes=48 * 1024 * 1024
        ),
        name="sampled_and_bases",
    )(
        *[
            a if a is ranks else pltpu.with_memory_space_constraint(a, pltpu.HBM)
            for a in (
                parent_tile,
                parent_front,
                column_tiles,
                ranks,
                slab,
                samples.reshape(-1, 128, width),
                child_tiles,
            )
        ]
    )


def sampled_and_gram_any(
    slab, samples, child_tiles, parent_front, parent_tile, column_tiles, ranks
):
    width = samples.shape[1]
    half = width // 2
    col_width = slab.shape[1]
    omega = lax.all_gather(samples, ("row", "col"), axis=0, tiled=True)
    own = lax.dynamic_slice_in_dim(omega, lax.axis_index("col") * col_width, col_width, 0)
    direct = lax.psum_scatter(
        jnp.dot(slab, own, preferred_element_type=F32), "col", scatter_dimension=0, tiled=True
    )
    count = child_tiles.shape[0]
    blocks = child_tiles.shape[2] // 128
    chosen = omega.reshape(-1, 128, width)[column_tiles]
    pieces = child_tiles.reshape(count, 128, blocks, 128)
    product = jnp.einsum("trkc,tkcs->trs", pieces, chosen, preferred_element_type=F32)
    row_tiles = slab.shape[0] * lax.axis_size("row") // 128
    label = (parent_front[:, 0] * row_tiles + parent_tile).astype(F32)
    product = lax.all_gather(product, "front", axis=0, tiled=True)
    label = lax.all_gather(label, "front", axis=0, tiled=True)
    wanted = (lax.axis_index("front") * row_tiles + jnp.arange(row_tiles)).astype(F32)
    spread = (label[:, None] == wanted[None, :]).astype(F32)
    rows_full = jnp.einsum("qj,qrs->jrs", spread, product, precision=HI)
    rows_full = rows_full.reshape(row_tiles * 128, width)
    extended = lax.psum_scatter(rows_full, ("row", "col"), scatter_dimension=0, tiled=True)
    sampled = direct + extended
    masked = jnp.where(jnp.arange(width)[None, :] < ranks[0, 0], sampled, 0.0)
    gram = lax.psum(jnp.dot(masked.T, masked, precision=HI), "col")
    gram = jnp.stack([gram[:half, :half], gram[half:, :half], gram[half:, half:]])
    rank = jnp.broadcast_to(ranks.astype(F32)[:, :, None], (3, 8, half))
    return sampled, jnp.concatenate([gram, rank], axis=1)


def on_device(
    sizes, front_slab, samples, child_tiles, parent_front, parent_tile, column_tiles, ranks
):
    args = (samples, child_tiles, parent_front, parent_tile, column_tiles, ranks)
    tiles, count = samples.shape[0] // 128, child_tiles.shape[0]
    near = sizes["row"] == 4 and sizes["col"] == 2 and sizes["front"] == 4
    if near and tiles % 8 == 0 and count == 2 and front_slab.shape[1] == 512:
        sampled, basis = sampled_and_bases(front_slab[0], *args)
    else:
        sampled, gram = sampled_and_gram_any(front_slab[0], *args)
        sampled, basis = leaf_bases(sampled, gram)
    return (sampled[None], basis[None])


def solution(mesh):
    in_specs = (
        P("front", "row", "col"),
        P(("row", "col"), None),
        P(("front", "row", "col"), None, None),
        P(("front", "row", "col"), None),
        P(("front", "row", "col")),
        P(("front", "row", "col"), None),
        P("front", "row"),
    )
    out_specs = (P("front", ("row", "col"), None), P("front", ("row", "col"), None))
    return jax.shard_map(
        functools.partial(on_device, dict(mesh.shape)),
        mesh=mesh,
        in_specs=in_specs,
        out_specs=out_specs,
        check_vma=False,
    )
```
